512 devices in a mesh: gx: 32 (over x, y), gy: 16 (over z, core).
Axes of the slice: x: 4, y: 8, z: 8, core: 2. Of those that a mesh axis runs over, the one named last changes fastest.
Arguments:
- cotangent: float32 [256, 128, 512], P('gx', 'gy'), may hold values from -8 to 8
- concentration: float32 [256, 128, 512], P('gx', 'gy'), may hold values from 0.5 to 2
- conductance: float32 [256, 128, 16], P('gx', 'gy'), may hold values from 0.5 to 2
- diffusivity: float32 [32], replicated, may hold values from 30 to 10000
- rate_constant: float32 [256], replicated, may hold values from 0.02 to 0.3
- reactants: int32 [256, 2], replicated, may hold values from 0 to 31
- products: int32 [256, 2], replicated, may hold values from 0 to 31
Outputs:
- sensitivity: float32 [256, 128, 512], P('gx', 'gy')
The draws below stay inside these ranges and needn't reach their ends.
All inputs are finite; a program needn't handle non-finite values.
Results may differ from the reference program's by a relative error of at most 0.0003.
Values sent between devices are 32-bit elements; how exact they have to be, the bound alone decides.
No kernel may reach another device: no remote copies, remote signals or barrier semaphores. Data moves between devices by JAX's collectives and lax.ppermute only.
A program may use at most 64 MiB of HBM per device.

```python
import math
import jax
import jax.numpy as jnp
from jax import lax

S = 32
REACT = 256
NZ = 16
NX = 256
NY = 128


def draw_cotangent(key, part):
    random_part = jax.random.normal(key, (NX, NY, S * NZ), jnp.float32)
    return jnp.clip(random_part, -8.0, 8.0)


def touch_ends(values, stream_key, least, top_value):
    shape = values.shape
    place = [jax.random.randint(jax.random.fold_in(stream_key, axis), (), 0, shape[axis]) for axis in range(len(shape))]
    values = values.at[tuple(place)].set(least)
    longest = shape.index(max(shape))
    place[longest] = (place[longest] + 1) % shape[longest]
    return values.at[tuple(place)].set(top_value)


def block_scale(stream_key, shape, shards, smallest, top_value):
    def one(axis_at, parts):
        heights = jax.random.uniform(jax.random.fold_in(jax.random.fold_in(stream_key, 6), axis_at), (parts,), jnp.float32, smallest / len(shards), top_value / len(shards))
        return jnp.repeat(jnp.exp(heights), shape[axis_at] // parts).reshape((-1,) + (1,) * (len(shape) - axis_at - 1))

    loudness = one(*shards[0])
    for cut in shards[1:]:
        loudness = loudness * one(*cut)
    return loudness


def setup_inputs(seed: int = 0) -> dict:
    splits = jax.random.split(jax.random.key(seed), 8)
    cotangent = draw_cotangent(jax.random.fold_in(splits[7], 71), 0)
    concentration = jnp.clip(jnp.exp(math.log(2.0) - 1.3862944 * jax.random.uniform(splits[1], (NX, NY, S * NZ), jnp.float32) ** block_scale(splits[1], (NX, NY, S * NZ), ((0, 32), (1, 16)), -0.2, 0.2)), 0.5, 2.0)
    conductance = jnp.clip(jnp.exp(math.log(2.0) - 1.3862944 * jax.random.uniform(splits[2], (NX, NY, NZ), jnp.float32) ** block_scale(splits[2], (NX, NY, NZ), ((0, 32), (1, 16)), -0.2, 0.2)), 0.5, 2.0)
    diffusivity = jnp.clip(jnp.exp(jax.random.uniform(splits[3], (S,), jnp.float32, math.log(30.0), math.log(10000.0))), 30.0, 10000.0)
    rate_constant = jnp.clip(jnp.exp(jax.random.uniform(splits[4], (REACT,), jnp.float32, math.log(0.02), math.log(0.3))), 0.02, 0.3)
    reactants = touch_ends(jax.random.randint(splits[5], (REACT, 2), 0, S), jax.random.fold_in(splits[5], 1), 0, S - 1).astype(jnp.int32)
    products = touch_ends(jax.random.randint(splits[6], (REACT, 2), 0, S), jax.random.fold_in(splits[6], 1), 0, S - 1).astype(jnp.int32)
    return dict(cotangent=cotangent, concentration=concentration, conductance=conductance, diffusivity=diffusivity, rate_constant=rate_constant, reactants=reactants, products=products)


def stoichiometry(reactants, products, species):
    species_ids = jnp.arange(species, dtype=jnp.int32)
    reactant_matrix = jnp.sum((reactants[:, :, None] == species_ids[None, None, :]).astype(jnp.float32), axis=1)
    product_matrix = jnp.sum((products[:, :, None] == species_ids[None, None, :]).astype(jnp.float32), axis=1)
    return reactant_matrix, product_matrix - reactant_matrix


def chem_adjoint(field, concentration, rate_constant, reactant_matrix, net_matrix):
    highest = lax.Precision.HIGHEST
    exponent = jnp.einsum('csz,rs->czr', jnp.log(concentration), reactant_matrix, precision=highest)
    rates = rate_constant * jnp.exp(exponent)
    inverse = 1.0 / concentration

    def transposed(vector):
        flows = jnp.einsum('csz,rs->czr', vector, net_matrix, precision=highest) * rates
        return jnp.einsum('czr,rs->csz', flows, reactant_matrix, precision=highest) * inverse

    third = field + transposed(field) / 3.0
    second = field + transposed(third) / 2.0
    return field + transposed(second)


def solve_lines(source, coefficient):
    diagonal = 1.0 + 2.0 * coefficient
    below = -jnp.concatenate([jnp.zeros_like(coefficient[:1]), coefficient[:-1]], axis=0)
    above = -jnp.concatenate([coefficient[1:], jnp.zeros_like(coefficient[:1])], axis=0)

    def forward(carry, row_data):
        ratio_prev, value_prev = carry
        sub_row, diag_row, super_row, source_row = row_data
        denominator = diag_row - sub_row * ratio_prev
        ratio_now = super_row / denominator
        value_now = (source_row - sub_row * value_prev) / denominator
        return (ratio_now, value_now), (ratio_now, value_now)

    initial = (jnp.zeros_like(source[0]), jnp.zeros_like(source[0]))
    final_carry, stacked = lax.scan(forward, initial, (below, diagonal, above, source))

    def backward(later_cell, row_data):
        ratio_now, value_now = row_data
        current = value_now - ratio_now * later_cell
        return current, current

    last_carry, solution = lax.scan(backward, jnp.zeros_like(source[0]), stacked, reverse=True)
    return solution


def reference(cotangent, concentration, conductance, diffusivity, rate_constant, reactants, products):
    coefficient = (conductance[:, :, None, :] * diffusivity[None, None, :, None]).reshape(NX, NY, S * NZ)
    after_y = jnp.moveaxis(solve_lines(jnp.moveaxis(cotangent, 1, 0), jnp.moveaxis(coefficient, 1, 0)), 0, 1)
    reactant_matrix, net_matrix = stoichiometry(reactants, products, S)

    def chem_row(paired):
        field_row, conc_row = paired
        result = chem_adjoint(field_row.reshape(NY, S, NZ), conc_row.reshape(NY, S, NZ), rate_constant, reactant_matrix, net_matrix)
        return result.reshape(NY, S * NZ)

    after_chem = lax.map(chem_row, (after_y, concentration))
    return solve_lines(after_chem, coefficient)
```

```python
import functools

import jax
import jax.numpy as jnp
from jax import lax
from jax.experimental import pallas as pl
from jax.experimental.pallas import tpu as pltpu
from jax.sharding import PartitionSpec as P


CELLS = 8
LANES = 128


def call(kernel, out_shape, scratch_shapes=()):
    whole = pl.BlockSpec(memory_space=pltpu.VMEM)

    def run(*operands):
        outs = jax.tree.map(lambda _: whole, out_shape)
        return pl.pallas_call(
            kernel,
            out_shape=out_shape,
            in_specs=[whole] * len(operands),
            out_specs=outs,
            scratch_shapes=list(scratch_shapes),
        )(*operands)

    return run


def struct(*shape):
    return jax.ShapeDtypeStruct(shape, jnp.float32)


def spread(packed, cell, depth):
    lane = lax.broadcasted_iota(jnp.int32, packed.shape, 1)
    index = lax.rem(lane, depth) + cell * depth
    return jnp.take_along_axis(packed, index, axis=1, mode="promise_in_bounds")


def wide(tile, width):
    return jnp.concatenate([tile] * (width // LANES), axis=1)


def expand_all(gathered_ref, tiles_ref, blocks, depth):
    def body(block, carry):
        packed = 1.0 / gathered_ref[block]
        for cell in range(CELLS):
            tiles_ref[block * CELLS + cell] = spread(packed, cell, depth)
        return carry

    lax.fori_loop(0, blocks, body, 0)


def shoot(tiles_ref, inverse_rate, left_ref, left_step_ref, right_ref, right_step_ref, blocks):
    width = inverse_rate.shape[1]
    ones = jnp.ones_like(inverse_rate)

    def body(block, carry):
        left, left_step, right, right_step = carry
        mirror = blocks - 1 - block
        left_ref[block] = left
        left_step_ref[block] = left_step
        right_ref[mirror] = right
        right_step_ref[mirror] = right_step
        for cell in range(CELLS):
            ahead = wide(tiles_ref[block * CELLS + cell], width) * inverse_rate
            behind = wide(tiles_ref[mirror * CELLS + CELLS - 1 - cell], width) * inverse_rate
            left_step = left_step + ahead * left
            left = left + left_step
            right_step = right_step + behind * right
            right = right + right_step
        return left, left_step, right, right_step

    left, _, right, _ = lax.fori_loop(0, blocks, body, (ones, ones, ones, ones))
    left_ref[blocks] = left
    right_ref[blocks] = right


def own_block(tiles_ref, inverse_rate, left_ref, left_step_ref, right_ref, right_step_ref, me):
    width = inverse_rate.shape[1]
    rates = [wide(tiles_ref[me * CELLS + cell], width) * inverse_rate for cell in range(CELLS)]

    def sweep(value, step, order):
        ratios, gaps = [None] * CELLS, [None] * CELLS
        reciprocal = 1.0 / value
        for cell in order:
            gaps[cell] = step * reciprocal
            step = step + rates[cell] * value
            following = value + step
            reciprocal = 1.0 / following
            ratios[cell] = value * reciprocal
            value = following
        return ratios, gaps

    forward, left_gaps = sweep(left_ref[me], left_step_ref[me], range(CELLS))
    backward, right_gaps = sweep(right_ref[me], right_step_ref[me], reversed(range(CELLS)))
    gains = [
        rates[cell] / (rates[cell] + left_gaps[cell] + right_gaps[cell]) for cell in range(CELLS)
    ]
    return forward, backward, gains


def sweeps(sources, forward, backward, from_left, from_right):
    before, after = [None] * CELLS, [None] * CELLS
    running = from_left
    for cell in range(CELLS):
        before[cell] = running
        running = forward[cell] * (sources[cell] + running)
    last = running
    running = from_right
    for cell in reversed(range(CELLS)):
        after[cell] = running
        running = backward[cell] * (sources[cell] + running)
    return before, after, last, running


def start_kernel(depth, members, cot_ref, cond_ref, inverse_ref, send_ref, lines_ref):
    width = cot_ref.shape[2]
    inverse_rate = jnp.broadcast_to(inverse_ref[...], (CELLS, width))
    packed = 1.0 / cond_ref[...]
    lines = jnp.swapaxes(cot_ref[...], 0, 1)
    lines_ref[...] = lines
    sources = [lines[cell] for cell in range(CELLS)]
    rates = [wide(spread(packed, cell, depth), width) * inverse_rate for cell in range(CELLS)]

    def project(order):
        value = jnp.ones_like(inverse_rate)
        step = value
        total = jnp.zeros_like(value)
        for cell in order:
            total = total + value * sources[cell]
            step = step + rates[cell] * value
            value = value + step
        return total / value

    last = project(range(CELLS))
    first = project(reversed(range(CELLS)))
    for member in range(members):
        send_ref[member, :, :width] = first
        send_ref[member, :, width : 2 * width] = last
        send_ref[member, :, 2 * width :] = cond_ref[...]


def to_species(cells, turn_ref, depth):
    rows = cells.shape[0]
    turn_ref[...] = jnp.concatenate([cells, cells], axis=0).T
    species = cells.shape[1] // depth
    low = lax.broadcasted_iota(jnp.int32, (species, 2 * rows), 1) < rows
    pairs = []
    for pair in range(depth // 2):
        even = turn_ref[pl.ds(2 * pair, species, stride=depth), :]
        odd = turn_ref[pl.ds(2 * pair + 1, species, stride=depth), :]
        pairs.append(jnp.where(low, even, odd))
    return pairs


def from_species(pairs, turn_ref, depth):
    species, columns = pairs[0].shape
    for pair, tile in enumerate(pairs):
        turn_ref[pl.ds(2 * pair, species, stride=depth), :] = tile
        turn_ref[pl.ds(2 * pair + 1, species, stride=depth), :] = pltpu.roll(
            tile, columns // 2, 1
        )
    return turn_ref[...].T[: columns // 2]


def halves(value):
    high = value.astype(jnp.bfloat16)
    return high, (value - high.astype(jnp.float32)).astype(jnp.bfloat16)


def counts(pair_ref, species):
    ids = lax.broadcasted_iota(jnp.int32, (pair_ref.shape[0], species), 1)
    return (pair_ref[:, 0:1] == ids).astype(jnp.float32) + (pair_ref[:, 1:2] == ids).astype(
        jnp.float32
    )


def rates_kernel(
    depth, conc_ref, rate_ref, reactants_ref, products_ref, rates_ref, inverse_ref, net_ref,
    back_ref, turn_ref,
):
    rows_x, rows_y, width = conc_ref.shape
    species = width // depth
    used = counts(reactants_ref, species)
    net = (counts(products_ref, species) - used).astype(jnp.bfloat16)
    net_ref[...] = jnp.concatenate([net, net], axis=1)
    back_ref[...] = used.T.astype(jnp.bfloat16)
    used = used.astype(jnp.bfloat16)
    used = jnp.concatenate([used, used], axis=1)
    constant = rate_ref[...]
    pairs = to_species(conc_ref[...].reshape(rows_x * rows_y, width), turn_ref, depth)
    for pair, conc in enumerate(pairs):
        columns = pl.ds(pair * conc.shape[1], conc.shape[1])
        inverse_ref[:, columns] = 1.0 / conc
        stacked = jnp.concatenate(halves(jnp.log(conc)), axis=0)
        exponent = jnp.dot(used, stacked, preferred_element_type=jnp.float32)
        rates_ref[:, columns] = constant * jnp.exp(exponent)


def chemistry(field, rates, inverse, net, back):
    def transposed(vector):
        stacked = jnp.concatenate(halves(vector), axis=0)
        flows = jnp.dot(net, stacked, preferred_element_type=jnp.float32) * rates
        high, low = halves(flows)
        gathered = jnp.dot(back, high, preferred_element_type=jnp.float32) + jnp.dot(
            back, low, preferred_element_type=jnp.float32
        )
        return gathered * inverse

    third = field + transposed(field) * (1.0 / 3.0)
    second = field + transposed(third) * 0.5
    return field + transposed(second)


def weights_kernel(
    depth, blocks, axis, gathered_ref, inverse_ref, weight_ref, forward_ref, backward_ref,
    gain_ref, tiles_ref, left_ref, left_step_ref, right_ref, right_step_ref,
):
    me = lax.axis_index(axis)
    width = inverse_ref.shape[1]
    inverse_rate = jnp.broadcast_to(inverse_ref[...], (CELLS, width))
    expand_all(gathered_ref, tiles_ref, blocks, depth)
    shoot(tiles_ref, inverse_rate, left_ref, left_step_ref, right_ref, right_step_ref, blocks)
    left_scale = 1.0 / left_ref[me]
    right_scale = 1.0 / right_ref[me]

    def lower(block, carry):
        weight_ref[block] = left_ref[block + 1] * left_scale
        return carry

    def upper(block, carry):
        weight_ref[block] = right_ref[block - 1] * right_scale
        return carry

    lax.fori_loop(0, me, lower, 0)
    lax.fori_loop(me + 1, blocks, upper, 0)
    weight_ref[me] = jnp.zeros_like(left_scale)
    forward, backward, gains = own_block(
        tiles_ref, inverse_rate, left_ref, left_step_ref, right_ref, right_step_ref, me
    )
    for cell in range(CELLS):
        forward_ref[cell] = forward[cell]
        backward_ref[cell] = backward[cell]
        gain_ref[cell] = gains[cell]


def middle_kernel(
    depth, blocks, axis, next_blocks, next_axis, received_ref, lines_ref, inverse_ref, rates_ref,
    inverse_conc_ref, net_ref, back_ref, forward_ref, backward_ref, send_ref, sources_ref,
    cond_ref, tiles_ref, left_ref, left_step_ref, right_ref, right_step_ref, turn_ref,
):
    me = lax.axis_index(axis)
    width = inverse_ref.shape[1]
    inverse_rate = jnp.broadcast_to(inverse_ref[...], (CELLS, width))
    cond_ref[...] = received_ref[:, :, 2 * width :]
    expand_all(cond_ref, tiles_ref, blocks, depth)
    shoot(tiles_ref, inverse_rate, left_ref, left_step_ref, right_ref, right_step_ref, blocks)

    def lower(block, total):
        first = received_ref[block, :, :width]
        last = received_ref[block, :, width : 2 * width]
        outside = left_ref[block] - left_step_ref[block]
        return total + outside * first + left_ref[block + 1] * last

    def upper(block, total):
        first = received_ref[block, :, :width]
        last = received_ref[block, :, width : 2 * width]
        outside = right_ref[block] - right_step_ref[block]
        return total + right_ref[block - 1] * first + outside * last

    zero = jnp.zeros_like(inverse_rate)
    from_left = lax.fori_loop(0, me, lower, zero) / left_ref[me]
    from_right = lax.fori_loop(me + 1, blocks, upper, zero) / right_ref[me]
    forward, backward, gains = own_block(
        tiles_ref, inverse_rate, left_ref, left_step_ref, right_ref, right_step_ref, me
    )
    sources = [lines_ref[cell] for cell in range(CELLS)]
    before, after, _, _ = sweeps(sources, forward, backward, from_left, from_right)
    solved = jnp.stack(
        [(sources[k] + before[k] + after[k]) * gains[k] for k in range(CELLS)], axis=0
    )
    solved = jnp.swapaxes(solved, 0, 1).reshape(CELLS * CELLS, width)

    net = net_ref[...]
    back = back_ref[...]
    pairs = to_species(solved, turn_ref, depth)
    columns = pairs[0].shape[1]
    done = []
    for chunk in range(len(pairs) // 2):
        at = pl.ds(chunk * 2 * columns, 2 * columns)
        field = jnp.concatenate(pairs[2 * chunk : 2 * chunk + 2], axis=1)
        result = chemistry(field, rates_ref[:, at], inverse_conc_ref[:, at], net, back)
        done += [result[:, :columns], result[:, columns:]]
    changed = from_species(done, turn_ref, depth).reshape(CELLS, CELLS, width)
    sources_ref[...] = changed
    _, _, last, first = sweeps(
        [changed[k] for k in range(CELLS)],
        [forward_ref[k] for k in range(CELLS)],
        [backward_ref[k] for k in range(CELLS)],
        zero,
        zero,
    )
    here = lax.axis_index(next_axis)

    def to_earlier(block, carry):
        send_ref[block] = first
        return carry

    def to_later(block, carry):
        send_ref[block] = last
        return carry

    lax.fori_loop(0, here + 1, to_earlier, 0)
    lax.fori_loop(here + 1, next_blocks, to_later, 0)


def finish_kernel(
    blocks, axis, received_ref, weight_ref, sources_ref, forward_ref, backward_ref, gain_ref,
    out_ref,
):
    me = lax.axis_index(axis)
    zero = jnp.zeros_like(weight_ref[0])

    def add(block, total):
        return total + weight_ref[block] * received_ref[block]

    from_left = lax.fori_loop(0, me, add, zero)
    from_right = lax.fori_loop(me + 1, blocks, add, zero)
    sources = [sources_ref[k] for k in range(CELLS)]
    before, after, _, _ = sweeps(
        sources,
        [forward_ref[k] for k in range(CELLS)],
        [backward_ref[k] for k in range(CELLS)],
        from_left,
        from_right,
    )
    for k in range(CELLS):
        out_ref[k] = (sources[k] + before[k] + after[k]) * gain_ref[k]


def on_device(
    cotangent, concentration, conductance, diffusivity, rate_constant, reactants, products
):
    rows_x, rows_y, width = cotangent.shape
    depth = conductance.shape[2]
    species = diffusivity.shape[0]
    reactions = rate_constant.shape[0]
    across_x = lax.axis_size("gx")
    across_y = lax.axis_size("gy")
    packed_y = conductance.reshape(rows_x, rows_y * depth)
    packed_x = jnp.swapaxes(conductance, 0, 1).reshape(rows_y, rows_x * depth)
    inverse_rate = jnp.repeat(1.0 / diffusivity, depth)[None, :]

    def shots(blocks):
        edge = pltpu.VMEM((blocks + 1, CELLS, width), jnp.float32)
        return [pltpu.VMEM((blocks * CELLS, CELLS, LANES), jnp.float32)] + [edge] * 4

    turn = pltpu.VMEM((width, 2 * rows_x * rows_y), jnp.float32)
    block = struct(CELLS, CELLS, width)

    gathered_x = lax.all_to_all(
        jnp.broadcast_to(packed_x, (across_x, rows_y, rows_x * depth)), "gx", 0, 0, tiled=True
    )
    send_y, lines = call(
        functools.partial(start_kernel, depth, across_y),
        [struct(across_y, CELLS, 2 * width + LANES), block],
    )(cotangent, packed_y, inverse_rate)
    received_y = lax.all_to_all(send_y, "gy", 0, 0, tiled=True)
    rates, inverse_conc, net, back = call(
        functools.partial(rates_kernel, depth),
        [
            struct(reactions, rows_x * rows_y * depth),
            struct(species, rows_x * rows_y * depth),
            jax.ShapeDtypeStruct((reactions, 2 * species), jnp.bfloat16),
            jax.ShapeDtypeStruct((species, reactions), jnp.bfloat16),
        ],
        [turn],
    )(concentration, rate_constant[:, None], reactants, products)
    weight, forward, backward, gain = call(
        functools.partial(weights_kernel, depth, across_x, "gx"),
        [struct(across_x, CELLS, width), block, block, block],
        shots(across_x),
    )(gathered_x, inverse_rate)
    send_x, sources = call(
        functools.partial(middle_kernel, depth, across_y, "gy", across_x, "gx"),
        [struct(across_x, CELLS, width), block],
        [pltpu.VMEM((across_y, CELLS, LANES), jnp.float32)] + shots(across_y) + [turn],
    )(received_y, lines, inverse_rate, rates, inverse_conc, net, back, forward, backward)
    received_x = lax.all_to_all(send_x, "gx", 0, 0, tiled=True)
    return call(functools.partial(finish_kernel, across_x, "gx"), block)(
        received_x, weight, sources, forward, backward, gain
    )


def solution(mesh):
    placed = (P("gx", "gy", None), P("gx", "gy", None), P("gx", "gy", None), P(), P(), P(), P())
    return jax.shard_map(
        on_device, mesh=mesh, in_specs=placed, out_specs=P("gx", "gy", None), check_vma=False
    )
```

```python
import functools

import jax
import jax.numpy as jnp
from jax import lax
from jax.experimental import pallas as pl
from jax.experimental.pallas import tpu as pltpu
from jax.sharding import PartitionSpec as P


CELLS = 8
LANES = 128
ROWS = 8
LIMIT = 16 << 20


def call(kernel, out_shape, scratch_shapes=()):
    whole = pl.BlockSpec(memory_space=pltpu.VMEM)

    def run(*operands):
        outs = jax.tree.map(lambda _: whole, out_shape)
        return pl.pallas_call(
            kernel,
            out_shape=out_shape,
            in_specs=[whole] * len(operands),
            out_specs=outs,
            scratch_shapes=list(scratch_shapes),
            compiler_params=pltpu.CompilerParams(vmem_limit_bytes=LIMIT),
        )(*operands)

    return run


def struct(*shape):
    return jax.ShapeDtypeStruct(shape, jnp.float32)


def cell_rates(cond, diffusivity, width, depth):
    lane = lax.broadcasted_iota(jnp.int32, (depth, width), 1)
    same_depth = lax.rem(lane, depth) == lax.broadcasted_iota(jnp.int32, (depth, width), 0)
    species = width // depth
    lane = lax.broadcasted_iota(jnp.int32, (species, width), 1)
    same_species = lax.div(lane, depth) == lax.broadcasted_iota(jnp.int32, (species, width), 0)
    highest = lax.Precision.HIGHEST
    spread = jnp.dot(
        (1.0 / cond).reshape(-1, depth),
        same_depth.astype(jnp.float32),
        precision=highest,
        preferred_element_type=jnp.float32,
    )
    scale = jnp.dot(
        jnp.broadcast_to(1.0 / diffusivity, (CELLS, species)),
        same_species.astype(jnp.float32),
        precision=highest,
        preferred_element_type=jnp.float32,
    )
    tiles = spread.reshape(CELLS, CELLS, width)
    return [tiles[cell] * scale for cell in range(CELLS)]


def factors(rates):
    one = jnp.ones_like(rates[0])
    zero = jnp.zeros_like(one)

    def shoot(value, step, order):
        values = {}
        for cell in order:
            values[cell] = value
            step = step + rates[cell] * value
            value = value + step
        return values, value, step

    flat, flat_out, flat_step = shoot(one, zero, range(CELLS))
    slope, slope_out, slope_step = shoot(zero, one, range(CELLS))
    right, _, _ = shoot(one, one, reversed(range(CELLS)))
    inverse = 1.0 / (flat_out + slope_out)
    to_last = [(flat[k] + slope[k]) * inverse for k in range(CELLS)]
    to_first = [right[k] * inverse for k in range(CELLS)]
    transfer = (flat_step, slope_step, flat[CELLS - 1], slope[CELLS - 1])
    return to_first, to_last, transfer


def local_solution(sources, rates, to_first, to_last):
    first, last = to_first[0] * 0.0, None
    before, after = [None] * CELLS, [None] * CELLS
    running = first
    for k in range(CELLS):
        before[k] = running
        if k < CELLS - 1:
            running = (to_last[k] / to_last[k + 1]) * (sources[k] + running)
    running = first
    for k in reversed(range(CELLS)):
        after[k] = running
        if k > 0:
            running = (to_first[k] / to_first[k - 1]) * (sources[k] + running)
    return [
        (sources[k] + before[k] + after[k]) * (to_first[k] * to_last[k] / to_first[CELLS - 1])
        for k in range(CELLS)
    ]


def total(weights, sources):
    terms = [weight * source for weight, source in zip(weights, sources, strict=True)]
    while len(terms) > 1:
        terms = [a + b for a, b in zip(terms[::2], terms[1::2], strict=True)]
    return terms[0]


def put_rows(send_ref, rows):
    for row, value in enumerate(rows):
        for tile in range(value.shape[1] // LANES):
            send_ref[pl.ds(tile * ROWS + row, CELLS, stride=CELLS * 4), :] = value[
                :, tile * LANES : (tile + 1) * LANES
            ]


def get_ends(back_ref):
    return [
        jnp.concatenate(
            [back_ref[pl.ds(tile * 2 + side, CELLS, stride=CELLS), :] for tile in range(4)], axis=1
        )
        for side in range(2)
    ]


def start_kernel(depth, cot_ref, cond_ref, diffusivity_ref, send_ref):
    width = cot_ref.shape[2]
    lines = jnp.swapaxes(cot_ref[...], 0, 1)
    cond = jnp.swapaxes(cond_ref[...], 0, 1)
    sources = [lines[cell] for cell in range(CELLS)]
    rates = cell_rates(cond, diffusivity_ref[...], width, depth)
    to_first, to_last, transfer = factors(rates)
    blank = jnp.zeros_like(rates[0])
    put_rows(
        send_ref,
        [total(to_first, sources), total(to_last, sources), *transfer, blank, blank],
    )


def solve_kernel(blocks, tiles, got_ref, out_ref, *scratch):
    value_l, step_l, value_r, step_r, ratio_l, add_l, ratio_r, add_r, sum_l, sum_r = scratch
    one = jnp.ones((1, LANES), jnp.float32)

    def pick(block, tile, row):
        return got_ref[pl.ds((block * tiles + tile) * ROWS + row, 1), :]

    def whole(tile, row):
        return got_ref[pl.ds(tile * ROWS + row, blocks, stride=ROWS * tiles), :]

    for tile in range(tiles):
        left, left_step, right, right_step = one, one, one, one
        for block in range(blocks):
            mirror = blocks - 1 - block
            value_l[tile, pl.ds(block, 1), :] = left
            step_l[tile, pl.ds(block, 1), :] = left_step
            value_r[tile, pl.ds(mirror + 1, 1), :] = right
            step_r[tile, pl.ds(mirror + 1, 1), :] = right_step
            c, d, e, f = (pick(block, tile, row) for row in range(2, 6))
            kept = e * left + f * left_step
            left_step = c * left + d * left_step
            left = kept + left_step
            c, d, e, f = (pick(mirror, tile, row) for row in range(2, 6))
            kept = d * right + f * right_step
            right_step = c * right + e * right_step
            right = kept + right_step
        value_l[tile, pl.ds(blocks, 1), :] = left
        step_l[tile, pl.ds(blocks, 1), :] = left_step
        value_r[tile, pl.ds(0, 1), :] = right
        step_r[tile, pl.ds(0, 1), :] = right_step
    for tile in range(tiles):
        near = pl.ds(0, blocks)
        far = pl.ds(1, blocks)
        first, last = whole(tile, 0), whole(tile, 1)
        inverse = 1.0 / value_l[tile, far, :]
        at = value_l[tile, near, :]
        ratio_l[tile] = at * inverse
        add_l[tile] = last + (at - step_l[tile, near, :]) * inverse * first
        inverse = 1.0 / value_r[tile, near, :]
        at = value_r[tile, far, :]
        ratio_r[tile] = at * inverse
        add_r[tile] = first + (at - step_r[tile, far, :]) * inverse * last
    for tile in range(tiles):
        left = jnp.zeros_like(one)
        right = jnp.zeros_like(one)
        for block in range(blocks):
            mirror = blocks - 1 - block
            sum_l[tile, pl.ds(block, 1), :] = left
            sum_r[tile, pl.ds(mirror + 1, 1), :] = right
            here, there = pl.ds(block, 1), pl.ds(mirror, 1)
            left = ratio_l[tile, here, :] * left + add_l[tile, here, :]
            right = ratio_r[tile, there, :] * right + add_r[tile, there, :]
        sum_l[tile, pl.ds(blocks, 1), :] = left
        sum_r[tile, pl.ds(0, 1), :] = right
    for tile in range(tiles):
        for side in range(2):
            rows = pl.ds(side, blocks)
            gap_l = step_l[tile, rows, :] / value_l[tile, rows, :]
            gap_r = step_r[tile, rows, :] / value_r[tile, rows, :]
            inverse = 1.0 / (gap_l + gap_r * (1.0 - gap_l))
            left, right = sum_l[tile, rows, :], sum_r[tile, rows, :]
            if side == 0:
                ends = (left + (1.0 - gap_l) * right) * inverse
            else:
                ends = (right + (1.0 - gap_r) * left) * inverse
            out_ref[pl.ds(tile * 2 + side, blocks, stride=2 * tiles), :] = ends


def to_species(cells, turn_ref, depth):
    rows = cells.shape[0]
    turn_ref[...] = jnp.concatenate([cells, cells], axis=0).T
    species = cells.shape[1] // depth
    low = lax.broadcasted_iota(jnp.int32, (species, 2 * rows), 1) < rows
    pairs = []
    for pair in range(depth // 2):
        even = turn_ref[pl.ds(2 * pair, species, stride=depth), :]
        odd = turn_ref[pl.ds(2 * pair + 1, species, stride=depth), :]
        pairs.append(jnp.where(low, even, odd))
    return pairs


def from_species(pairs, turn_ref, depth):
    species, columns = pairs[0].shape
    for pair, tile in enumerate(pairs):
        turn_ref[pl.ds(2 * pair, species, stride=depth), :] = tile
        turn_ref[pl.ds(2 * pair + 1, species, stride=depth), :] = pltpu.roll(
            tile, columns // 2, 1
        )
    return turn_ref[...].T[: columns // 2]


def halves(value):
    high = value.astype(jnp.bfloat16)
    return high, (value - high.astype(jnp.float32)).astype(jnp.bfloat16)


def counts(pair_ref, species):
    ids = lax.broadcasted_iota(jnp.int32, (pair_ref.shape[0], species), 1)
    return (pair_ref[:, 0:1] == ids).astype(jnp.float32) + (pair_ref[:, 1:2] == ids).astype(
        jnp.float32
    )


def counts(pair_ref, species):
    ids = lax.broadcasted_iota(jnp.int32, (species, pair_ref.shape[1]), 0)
    return (pair_ref[0:1, :] == ids).astype(jnp.float32) + (pair_ref[1:2, :] == ids).astype(
        jnp.float32
    )


def prepare_kernel(
    depth, cot_ref, conc_ref, cond_ref, diffusivity_ref, rate_ref, reactants_ref, products_ref,
    rates_ref, inverse_ref, net_ref, back_ref, local_y_ref, first_y_ref, last_y_ref, first_x_ref,
    last_x_ref, transfer_ref, turn_ref,
):
    rows_x, rows_y, width = conc_ref.shape
    species = width // depth
    used = counts(reactants_ref, species)
    net = counts(products_ref, species) - used
    back_ref[...] = used.astype(jnp.bfloat16)
    net_ref[...] = jnp.concatenate([net, net], axis=0).T.astype(jnp.bfloat16)
    twice = jnp.concatenate([used, used], axis=0).T.astype(jnp.bfloat16)
    constant = jnp.broadcast_to(rate_ref[...], (LANES, rate_ref.shape[1])).T
    pairs = to_species(conc_ref[...].reshape(rows_x * rows_y, width), turn_ref, depth)
    for pair, conc in enumerate(pairs):
        columns = pl.ds(pair * conc.shape[1], conc.shape[1])
        inverse_ref[:, columns] = 1.0 / conc
        stacked = jnp.concatenate(halves(jnp.log(conc)), axis=0)
        exponent = jnp.dot(twice, stacked, preferred_element_type=jnp.float32)
        rates_ref[:, columns] = constant * jnp.exp(exponent)

    cond = cond_ref[...]
    rates = cell_rates(cond, diffusivity_ref[...], width, depth)
    to_first, to_last, transfer = factors(rates)
    for k in range(CELLS):
        first_x_ref[k] = to_first[k]
        last_x_ref[k] = to_last[k]
    for k in range(4):
        transfer_ref[k] = transfer[k]
    rates = cell_rates(jnp.swapaxes(cond, 0, 1), diffusivity_ref[...], width, depth)
    to_first, to_last, _ = factors(rates)
    lines = jnp.swapaxes(cot_ref[...], 0, 1)
    local = local_solution([lines[k] for k in range(CELLS)], rates, to_first, to_last)
    for k in range(CELLS):
        local_y_ref[k] = local[k] * rates[k]
        first_y_ref[k] = to_first[k] * rates[k]
        last_y_ref[k] = to_last[k] * rates[k]


def chemistry(field, rates, inverse, net, back):
    def transposed(vector):
        stacked = jnp.concatenate(halves(vector), axis=0)
        flows = jnp.dot(net, stacked, preferred_element_type=jnp.float32) * rates
        high, low = halves(flows)
        gathered = jnp.dot(back, high, preferred_element_type=jnp.float32) + jnp.dot(
            back, low, preferred_element_type=jnp.float32
        )
        return gathered * inverse

    third = field + transposed(field) * (1.0 / 3.0)
    second = field + transposed(third) * 0.5
    return field + transposed(second)


def middle_kernel(
    depth, ends_ref, local_ref, first_ref, last_ref, rates_ref, inverse_ref, net_ref, back_ref,
    first_x_ref, last_x_ref, transfer_ref, send_ref, sources_ref, turn_ref,
):
    width = local_ref.shape[2]
    left, right = get_ends(ends_ref)
    solved = jnp.stack(
        [local_ref[k] + first_ref[k] * left + last_ref[k] * right for k in range(CELLS)], axis=0
    )
    solved = jnp.swapaxes(solved, 0, 1).reshape(CELLS * CELLS, width)
    net = net_ref[...]
    back = back_ref[...]
    pairs = to_species(solved, turn_ref, depth)
    columns = pairs[0].shape[1]
    done = []
    for chunk in range(len(pairs) // 2):
        at = pl.ds(chunk * 2 * columns, 2 * columns)
        field = jnp.concatenate(pairs[2 * chunk : 2 * chunk + 2], axis=1)
        result = chemistry(field, rates_ref[:, at], inverse_ref[:, at], net, back)
        done += [result[:, :columns], result[:, columns:]]
    changed = from_species(done, turn_ref, depth).reshape(CELLS, CELLS, width)
    sources_ref[...] = changed
    sources = [changed[k] for k in range(CELLS)]
    blank = jnp.zeros_like(left)
    put_rows(
        send_ref,
        [
            total([first_x_ref[k] for k in range(CELLS)], sources),
            total([last_x_ref[k] for k in range(CELLS)], sources),
            *(transfer_ref[k] for k in range(4)),
            blank,
            blank,
        ],
    )


def finish_kernel(
    depth, ends_ref, cond_ref, diffusivity_ref, sources_ref, first_ref, last_ref, out_ref
):
    width = out_ref.shape[2]
    rates = cell_rates(cond_ref[...], diffusivity_ref[...], width, depth)
    to_first = [first_ref[k] for k in range(CELLS)]
    to_last = [last_ref[k] for k in range(CELLS)]
    local = local_solution([sources_ref[k] for k in range(CELLS)], rates, to_first, to_last)
    left, right = get_ends(ends_ref)
    for k in range(CELLS):
        out_ref[k] = (local[k] + to_first[k] * left + to_last[k] * right) * rates[k]


def exchange(rows, axis):
    members = lax.axis_size(axis)
    blocks = rows.reshape(members, rows.shape[0] // members, LANES)
    return lax.all_to_all(blocks, axis, 0, 0, tiled=True).reshape(rows.shape)


def solve_lines(send, axis):
    blocks = lax.axis_size(axis)
    tiles = send.shape[0] // (blocks * ROWS)
    states = pltpu.VMEM((tiles, blocks + CELLS, LANES), jnp.float32)
    terms = pltpu.VMEM((tiles, blocks, LANES), jnp.float32)
    ends = call(
        functools.partial(solve_kernel, blocks, tiles),
        struct(2 * blocks * tiles, LANES),
        [states] * 4 + [terms] * 4 + [states] * 2,
    )(exchange(send, axis))
    return exchange(ends, axis)


def on_device(
    cotangent, concentration, conductance, diffusivity, rate_constant, reactants, products
):
    rows_x, rows_y, width = cotangent.shape
    depth = conductance.shape[2]
    species = diffusivity.shape[0]
    reactions = rate_constant.shape[0]
    columns = rows_x * rows_y * depth
    diffusivity = diffusivity[None, :]
    turn = pltpu.VMEM((width, 2 * rows_x * rows_y), jnp.float32)
    block = struct(CELLS, CELLS, width)
    send = struct(CELLS * (width // LANES) * ROWS, LANES)

    send_y = call(functools.partial(start_kernel, depth), send)(
        cotangent, conductance, diffusivity
    )
    rates, inverse, net, back, local_y, first_y, last_y, first_x, last_x, transfer = call(
        functools.partial(prepare_kernel, depth),
        [
            struct(reactions, columns),
            struct(species, columns),
            jax.ShapeDtypeStruct((reactions, 2 * species), jnp.bfloat16),
            jax.ShapeDtypeStruct((species, reactions), jnp.bfloat16),
            block,
            block,
            block,
            block,
            block,
            struct(4, CELLS, width),
        ],
        [turn],
    )(
        cotangent,
        concentration,
        conductance,
        diffusivity,
        rate_constant[None, :],
        reactants.T,
        products.T,
    )
    ends_y = solve_lines(send_y, "gy")
    send_x, sources = call(functools.partial(middle_kernel, depth), [send, block], [turn])(
        ends_y, local_y, first_y, last_y, rates, inverse, net, back, first_x, last_x, transfer
    )
    ends_x = solve_lines(send_x, "gx")
    return call(functools.partial(finish_kernel, depth), block)(
        ends_x, conductance, diffusivity, sources, first_x, last_x
    )


def solution(mesh):
    placed = (P("gx", "gy", None), P("gx", "gy", None), P("gx", "gy", None), P(), P(), P(), P())
    return jax.shard_map(
        on_device, mesh=mesh, in_specs=placed, out_specs=P("gx", "gy", None), check_vma=False
    )
```

```python
import functools

import jax
import jax.numpy as jnp
from jax import lax
from jax.experimental import pallas as pl
from jax.experimental.pallas import tpu as pltpu
from jax.sharding import PartitionSpec as P


CELLS = 8
LANES = 128
ROWS = 8
LIMIT = 16 << 20


def call(kernel, out_shape, scratch_shapes=(), far_in=(), far_out=()):
    near = pl.BlockSpec(memory_space=pltpu.VMEM)
    far = pl.BlockSpec(memory_space=pltpu.HBM)

    def run(*operands):
        operands = [
            pltpu.with_memory_space_constraint(x, pltpu.HBM) if k in far_in else x
            for k, x in enumerate(operands)
        ]
        outs = near
        if isinstance(out_shape, list):
            outs = [far if k in far_out else near for k in range(len(out_shape))]
        return pl.pallas_call(
            kernel,
            out_shape=out_shape,
            in_specs=[far if k in far_in else near for k in range(len(operands))],
            out_specs=outs,
            scratch_shapes=list(scratch_shapes),
            compiler_params=pltpu.CompilerParams(vmem_limit_bytes=LIMIT),
        )(*operands)

    return run


def struct(*shape):
    return jax.ShapeDtypeStruct(shape, jnp.float32)


def cell_rates(cond, diffusivity, width, depth):
    lane = lax.broadcasted_iota(jnp.int32, (depth, width), 1)
    same_depth = lax.rem(lane, depth) == lax.broadcasted_iota(jnp.int32, (depth, width), 0)
    species = width // depth
    lane = lax.broadcasted_iota(jnp.int32, (species, width), 1)
    same_species = lax.div(lane, depth) == lax.broadcasted_iota(jnp.int32, (species, width), 0)
    highest = lax.Precision.HIGHEST
    spread = jnp.dot(
        (1.0 / cond).reshape(-1, depth),
        same_depth.astype(jnp.float32),
        precision=highest,
        preferred_element_type=jnp.float32,
    )
    scale = jnp.dot(
        jnp.broadcast_to(1.0 / diffusivity, (CELLS, species)),
        same_species.astype(jnp.float32),
        precision=highest,
        preferred_element_type=jnp.float32,
    )
    tiles = spread.reshape(CELLS, CELLS, width)
    return [tiles[cell] * scale for cell in range(CELLS)]


def factors(rates):
    one = jnp.ones_like(rates[0])
    zero = jnp.zeros_like(one)

    def shoot(value, step, order):
        values = {}
        for cell in order:
            values[cell] = value
            step = step + rates[cell] * value
            value = value + step
        return values, value, step

    flat, flat_out, flat_step = shoot(one, zero, range(CELLS))
    slope, slope_out, slope_step = shoot(zero, one, range(CELLS))
    right, _, _ = shoot(one, one, reversed(range(CELLS)))
    inverse = 1.0 / (flat_out + slope_out)
    to_last = [(flat[k] + slope[k]) * inverse for k in range(CELLS)]
    to_first = [right[k] * inverse for k in range(CELLS)]
    transfer = (flat_step, slope_step, flat[CELLS - 1], slope[CELLS - 1])
    return to_first, to_last, transfer


def sweep_factors(to_first, to_last):
    ratio = to_last[0] * 0.0
    forward = [to_last[k] / to_last[k + 1] for k in range(CELLS - 1)] + [ratio]
    backward = [ratio] + [to_first[k] / to_first[k - 1] for k in range(1, CELLS)]
    scale = 1.0 / to_first[CELLS - 1]
    gains = [to_first[k] * to_last[k] * scale for k in range(CELLS)]
    return forward, backward, gains


def local_solution(sources, forward, backward, gains):
    before, after = [None] * CELLS, [None] * CELLS
    running = sources[0] * 0.0
    for k in range(CELLS):
        before[k] = sources[k] + running
        running = forward[k] * before[k]
    running = sources[0] * 0.0
    for k in reversed(range(CELLS)):
        after[k] = running
        running = backward[k] * (sources[k] + running)
    return [(before[k] + after[k]) * gains[k] for k in range(CELLS)]


def total(weights, sources):
    terms = [weight * source for weight, source in zip(weights, sources, strict=True)]
    while len(terms) > 1:
        terms = [a + b for a, b in zip(terms[::2], terms[1::2], strict=True)]
    return terms[0]


def put_rows(send_ref, rows):
    for row, value in enumerate(rows):
        for tile in range(value.shape[1] // LANES):
            send_ref[pl.ds(tile * ROWS + row, CELLS, stride=CELLS * 4), :] = value[
                :, tile * LANES : (tile + 1) * LANES
            ]


def get_ends(back_ref):
    return [
        jnp.concatenate(
            [back_ref[pl.ds(tile * 2 + side, CELLS, stride=CELLS), :] for tile in range(4)], axis=1
        )
        for side in range(2)
    ]


def start_kernel(
    depth, cot_from, cond_from, diffusivity_from, send_ref, cot_ref, cond_ref, diffusivity_ref, sem
):
    width = cot_ref.shape[2]
    copies = [
        pltpu.make_async_copy(cond_from, cond_ref, sem.at[0]),
        pltpu.make_async_copy(diffusivity_from, diffusivity_ref, sem.at[1]),
        pltpu.make_async_copy(cot_from, cot_ref, sem.at[2]),
    ]
    for copy in copies:
        copy.start()
    for copy in copies:
        copy.wait()
    lines = jnp.swapaxes(cot_ref[...], 0, 1)
    cond = jnp.swapaxes(cond_ref[...], 0, 1)
    sources = [lines[cell] for cell in range(CELLS)]
    rates = cell_rates(cond, diffusivity_ref[...], width, depth)
    to_first, to_last, transfer = factors(rates)
    blank = jnp.zeros_like(rates[0])
    put_rows(
        send_ref,
        [total(to_first, sources), total(to_last, sources), *transfer, blank, blank],
    )


def solve_kernel(blocks, tiles, got_ref, out_ref, *scratch):
    value_l, step_l, value_r, step_r, ratio_l, add_l, ratio_r, add_r, sum_l, sum_r = scratch
    one = jnp.ones((1, LANES), jnp.float32)

    def pick(block, tile, row):
        return got_ref[pl.ds((block * tiles + tile) * ROWS + row, 1), :]

    def whole(tile, row):
        return got_ref[pl.ds(tile * ROWS + row, blocks, stride=ROWS * tiles), :]

    for tile in range(tiles):
        left, left_step, right, right_step = one, one, one, one
        for block in range(blocks):
            mirror = blocks - 1 - block
            value_l[tile, pl.ds(block, 1), :] = left
            step_l[tile, pl.ds(block, 1), :] = left_step
            value_r[tile, pl.ds(mirror + 1, 1), :] = right
            step_r[tile, pl.ds(mirror + 1, 1), :] = right_step
            c, d, e, f = (pick(block, tile, row) for row in range(2, 6))
            kept = e * left + f * left_step
            left_step = c * left + d * left_step
            left = kept + left_step
            c, d, e, f = (pick(mirror, tile, row) for row in range(2, 6))
            kept = d * right + f * right_step
            right_step = c * right + e * right_step
            right = kept + right_step
        value_l[tile, pl.ds(blocks, 1), :] = left
        step_l[tile, pl.ds(blocks, 1), :] = left_step
        value_r[tile, pl.ds(0, 1), :] = right
        step_r[tile, pl.ds(0, 1), :] = right_step
    for tile in range(tiles):
        near = pl.ds(0, blocks)
        far = pl.ds(1, blocks)
        first, last = whole(tile, 0), whole(tile, 1)
        inverse = 1.0 / value_l[tile, far, :]
        at = value_l[tile, near, :]
        ratio_l[tile] = at * inverse
        add_l[tile] = last + (at - step_l[tile, near, :]) * inverse * first
        inverse = 1.0 / value_r[tile, near, :]
        at = value_r[tile, far, :]
        ratio_r[tile] = at * inverse
        add_r[tile] = first + (at - step_r[tile, far, :]) * inverse * last
    for tile in range(tiles):
        left = jnp.zeros_like(one)
        right = jnp.zeros_like(one)
        for block in range(blocks):
            mirror = blocks - 1 - block
            sum_l[tile, pl.ds(block, 1), :] = left
            sum_r[tile, pl.ds(mirror + 1, 1), :] = right
            here, there = pl.ds(block, 1), pl.ds(mirror, 1)
            left = ratio_l[tile, here, :] * left + add_l[tile, here, :]
            right = ratio_r[tile, there, :] * right + add_r[tile, there, :]
        sum_l[tile, pl.ds(blocks, 1), :] = left
        sum_r[tile, pl.ds(0, 1), :] = right
    for tile in range(tiles):
        for side in range(2):
            rows = pl.ds(side, blocks)
            gap_l = step_l[tile, rows, :] / value_l[tile, rows, :]
            gap_r = step_r[tile, rows, :] / value_r[tile, rows, :]
            inverse = 1.0 / (gap_l + gap_r * (1.0 - gap_l))
            left, right = sum_l[tile, rows, :], sum_r[tile, rows, :]
            if side == 0:
                ends = (left + (1.0 - gap_l) * right) * inverse
            else:
                ends = (right + (1.0 - gap_r) * left) * inverse
            out_ref[pl.ds(tile * 2 + side, blocks, stride=2 * tiles), :] = ends


def to_species(cells, turn_ref, depth):
    rows = cells.shape[0]
    turn_ref[...] = jnp.concatenate([cells, cells], axis=0).T
    species = cells.shape[1] // depth
    low = lax.broadcasted_iota(jnp.int32, (species, 2 * rows), 1) < rows
    pairs = []
    for pair in range(depth // 2):
        even = turn_ref[pl.ds(2 * pair, species, stride=depth), :]
        odd = turn_ref[pl.ds(2 * pair + 1, species, stride=depth), :]
        pairs.append(jnp.where(low, even, odd))
    return pairs


def from_species(pairs, turn_ref, depth):
    species, columns = pairs[0].shape
    for pair, tile in enumerate(pairs):
        turn_ref[pl.ds(2 * pair, species, stride=depth), :] = tile
        turn_ref[pl.ds(2 * pair + 1, species, stride=depth), :] = pltpu.roll(
            tile, columns // 2, 1
        )
    return turn_ref[...].T[: columns // 2]


def halves(value):
    high = value.astype(jnp.bfloat16)
    return high, (value - high.astype(jnp.float32)).astype(jnp.bfloat16)


def counts(pair_ref, species):
    ids = lax.broadcasted_iota(jnp.int32, (pair_ref.shape[0], species), 1)
    return (pair_ref[:, 0:1] == ids).astype(jnp.float32) + (pair_ref[:, 1:2] == ids).astype(
        jnp.float32
    )


def counts(pair_ref, species):
    ids = lax.broadcasted_iota(jnp.int32, (species, pair_ref.shape[1]), 0)
    return (pair_ref[0:1, :] == ids).astype(jnp.float32) + (pair_ref[1:2, :] == ids).astype(
        jnp.float32
    )


def prepare_kernel(
    depth, cot_ref, conc_ref, cond_ref, diffusivity_ref, rate_ref, reactants_ref, products_ref,
    jacobian_to, inverse_ref, local_y_ref, ends_y_ref, ends_x_ref, sweep_x_ref, transfer_ref,
    turn_ref, rates_ref, pairs_ref, jacobian_ref, sem,
):
    rows_x, rows_y, width = conc_ref.shape
    species = width // depth
    used = counts(reactants_ref, species)
    net = counts(products_ref, species) - used
    for s in range(species):
        product = (net[s : s + 1, :] * used).astype(jnp.bfloat16)
        rows = pl.ds(s * species, species)
        pairs_ref[rows, : used.shape[1]] = product
        pairs_ref[rows, used.shape[1] :] = product
    twice = jnp.concatenate([used, used], axis=0).T.astype(jnp.bfloat16)
    constant = jnp.broadcast_to(rate_ref[...], (LANES, rate_ref.shape[1])).T
    pairs = to_species(conc_ref[...].reshape(rows_x * rows_y, width), turn_ref, depth)
    for pair, conc in enumerate(pairs):
        columns = pl.ds(pair * conc.shape[1], conc.shape[1])
        inverse_ref[:, columns] = 1.0 / conc
        stacked = jnp.concatenate(halves(jnp.log(conc)), axis=0)
        exponent = jnp.dot(twice, stacked, preferred_element_type=jnp.float32)
        rates_ref[:, columns] = jnp.concatenate(halves(constant * jnp.exp(exponent)), axis=0)
    wide = 2 * LANES
    copies = []
    for chunk in range(rates_ref.shape[1] // wide):
        columns = pl.ds(chunk * wide, wide)
        block = jnp.dot(pairs_ref[...], rates_ref[:, columns], preferred_element_type=jnp.float32)
        for part in range(2):
            jacobian_ref[2 * chunk + part] = block[:, part * LANES : (part + 1) * LANES]
        tiles = pl.ds(2 * chunk, 2)
        copies.append(
            pltpu.make_async_copy(jacobian_ref.at[tiles], jacobian_to.at[tiles], sem.at[chunk])
        )
        copies[-1].start()

    cond = cond_ref[...]
    rates = cell_rates(cond, diffusivity_ref[...], width, depth)
    to_first, to_last, transfer = factors(rates)
    forward, backward, gains = sweep_factors(to_first, to_last)
    for k in range(CELLS):
        ends_x_ref[0, k] = to_first[k]
        ends_x_ref[1, k] = to_last[k]
        sweep_x_ref[0, k] = forward[k]
        sweep_x_ref[1, k] = backward[k]
        sweep_x_ref[2, k] = gains[k] * rates[k]
        sweep_x_ref[3, k] = to_first[k] * rates[k]
        sweep_x_ref[4, k] = to_last[k] * rates[k]
    for k in range(4):
        transfer_ref[k] = transfer[k]
    rates = cell_rates(jnp.swapaxes(cond, 0, 1), diffusivity_ref[...], width, depth)
    to_first, to_last, _ = factors(rates)
    lines = jnp.swapaxes(cot_ref[...], 0, 1)
    local = local_solution(
        [lines[k] for k in range(CELLS)], *sweep_factors(to_first, to_last)
    )
    for k in range(CELLS):
        local_y_ref[k] = local[k] * rates[k]
        ends_y_ref[0, k] = to_first[k] * rates[k]
        ends_y_ref[1, k] = to_last[k] * rates[k]
    for copy in copies:
        copy.wait()


def chemistry(field, columns, jacobian_ref, inverse, vector_ref):
    species = field.shape[0]

    def transposed(vector):
        vector_ref[:, columns] = vector
        sums = [None] * 4
        for s in range(species):
            row = jnp.broadcast_to(vector_ref[pl.ds(s, 1), columns], vector.shape)
            term = row * jacobian_ref[pl.ds(s * species, species), :]
            sums[s % 4] = term if sums[s % 4] is None else sums[s % 4] + term
        return ((sums[0] + sums[1]) + (sums[2] + sums[3])) * inverse

    third = field + transposed(field) * (1.0 / 3.0)
    second = field + transposed(third) * 0.5
    return field + transposed(second)


def middle_kernel(
    depth, ends_ref, local_ref, ends_y_ref, jacobian_from, inverse_ref, ends_x_ref, transfer_ref,
    send_ref, sources_ref, turn_ref, vector_ref, jacobian_ref, sem,
):
    width = local_ref.shape[2]
    copies = [
        pltpu.make_async_copy(jacobian_from.at[tile], jacobian_ref.at[tile], sem.at[tile])
        for tile in range(jacobian_ref.shape[0])
    ]
    for copy in copies:
        copy.start()
    left, right = get_ends(ends_ref)
    solved = jnp.stack(
        [
            local_ref[k] + ends_y_ref[0, k] * left + ends_y_ref[1, k] * right
            for k in range(CELLS)
        ],
        axis=0,
    )
    solved = jnp.swapaxes(solved, 0, 1).reshape(CELLS * CELLS, width)
    pairs = to_species(solved, turn_ref, depth)
    done = []
    for pair, field in enumerate(pairs):
        columns = pl.ds(pair * field.shape[1], field.shape[1])
        copies[pair].wait()
        jacobian = jacobian_ref.at[pair]
        done.append(chemistry(field, columns, jacobian, inverse_ref[:, columns], vector_ref))
    changed = from_species(done, turn_ref, depth).reshape(CELLS, CELLS, width)
    sources_ref[...] = changed
    sources = [changed[k] for k in range(CELLS)]
    blank = jnp.zeros_like(left)
    put_rows(
        send_ref,
        [
            total([ends_x_ref[0, k] for k in range(CELLS)], sources),
            total([ends_x_ref[1, k] for k in range(CELLS)], sources),
            *(transfer_ref[k] for k in range(4)),
            blank,
            blank,
        ],
    )


def finish_kernel(ends_ref, sources_ref, sweep_ref, out_ref):
    local = local_solution(
        [sources_ref[k] for k in range(CELLS)],
        *([sweep_ref[part, k] for k in range(CELLS)] for part in range(3)),
    )
    left, right = get_ends(ends_ref)
    for k in range(CELLS):
        out_ref[k] = local[k] + sweep_ref[3, k] * left + sweep_ref[4, k] * right


def exchange(rows, axis):
    members = lax.axis_size(axis)
    blocks = rows.reshape(members, rows.shape[0] // members, LANES)
    return lax.all_to_all(blocks, axis, 0, 0, tiled=True).reshape(rows.shape)


def solve_lines(send, axis):
    blocks = lax.axis_size(axis)
    tiles = send.shape[0] // (blocks * ROWS)
    states = pltpu.VMEM((tiles, blocks + CELLS, LANES), jnp.float32)
    terms = pltpu.VMEM((tiles, blocks, LANES), jnp.float32)
    ends = call(
        functools.partial(solve_kernel, blocks, tiles),
        struct(2 * blocks * tiles, LANES),
        [states] * 4 + [terms] * 4 + [states] * 2,
    )(exchange(send, axis))
    return exchange(ends, axis)


def on_device(
    cotangent, concentration, conductance, diffusivity, rate_constant, reactants, products
):
    rows_x, rows_y, width = cotangent.shape
    depth = conductance.shape[2]
    species = diffusivity.shape[0]
    reactions = rate_constant.shape[0]
    columns = rows_x * rows_y * depth
    diffusivity = diffusivity[None, :]
    turn = pltpu.VMEM((width, 2 * rows_x * rows_y), jnp.float32)
    block = struct(CELLS, CELLS, width)
    send = struct(CELLS * (width // LANES) * ROWS, LANES)

    send_y = call(
        functools.partial(start_kernel, depth),
        send,
        [
            pltpu.VMEM(cotangent.shape, jnp.float32),
            pltpu.VMEM(conductance.shape, jnp.float32),
            pltpu.VMEM(diffusivity.shape, jnp.float32),
            pltpu.SemaphoreType.DMA((3,)),
        ],
        far_in=(0, 1, 2),
    )(cotangent, conductance, diffusivity)
    jacobian, inverse, local_y, ends_y, ends_x, sweep_x, transfer = call(
        functools.partial(prepare_kernel, depth),
        [
            struct(columns // LANES, species * species, LANES),
            struct(species, columns),
            block,
            struct(2, CELLS, CELLS, width),
            struct(2, CELLS, CELLS, width),
            struct(5, CELLS, CELLS, width),
            struct(4, CELLS, width),
        ],
        [
            turn,
            pltpu.VMEM((2 * reactions, columns), jnp.bfloat16),
            pltpu.VMEM((species * species, 2 * reactions), jnp.bfloat16),
            pltpu.VMEM((columns // LANES, species * species, LANES), jnp.float32),
            pltpu.SemaphoreType.DMA((columns // (2 * LANES),)),
        ],
        far_out=(0,),
    )(
        cotangent,
        concentration,
        conductance,
        diffusivity,
        rate_constant[None, :],
        reactants.T,
        products.T,
    )
    got_y = solve_lines(send_y, "gy")
    send_x, sources = call(
        functools.partial(middle_kernel, depth),
        [send, block],
        [
            turn,
            pltpu.VMEM((species, columns), jnp.float32),
            pltpu.VMEM((columns // LANES, species * species, LANES), jnp.float32),
            pltpu.SemaphoreType.DMA((columns // LANES,)),
        ],
        far_in=(3,),
    )(got_y, local_y, ends_y, jacobian, inverse, ends_x, transfer)
    got_x = solve_lines(send_x, "gx")
    return call(finish_kernel, block)(got_x, sources, sweep_x)


def solution(mesh):
    placed = (P("gx", "gy", None), P("gx", "gy", None), P("gx", "gy", None), P(), P(), P(), P())
    return jax.shard_map(
        on_device, mesh=mesh, in_specs=placed, out_specs=P("gx", "gy", None), check_vma=False
    )
```

```python
import functools

import jax
import jax.numpy as jnp
from jax import lax
from jax.experimental import pallas as pl
from jax.experimental.pallas import tpu as pltpu
from jax.sharding import PartitionSpec as P


CELLS = 8
LANES = 128
ROWS = 8
LIMIT = 16 << 20


def call(kernel, out_shape, scratch_shapes=(), far_in=(), far_out=()):
    near = pl.BlockSpec(memory_space=pltpu.VMEM)
    far = pl.BlockSpec(memory_space=pltpu.HBM)

    def run(*operands):
        operands = [
            pltpu.with_memory_space_constraint(x, pltpu.HBM) if k in far_in else x
            for k, x in enumerate(operands)
        ]
        outs = near
        if isinstance(out_shape, list):
            outs = [far if k in far_out else near for k in range(len(out_shape))]
        return pl.pallas_call(
            kernel,
            out_shape=out_shape,
            in_specs=[far if k in far_in else near for k in range(len(operands))],
            out_specs=outs,
            scratch_shapes=list(scratch_shapes),
            compiler_params=pltpu.CompilerParams(vmem_limit_bytes=LIMIT),
        )(*operands)

    return run


def struct(*shape):
    return jax.ShapeDtypeStruct(shape, jnp.float32)


def begin(pairs, sem):
    copies = [pltpu.make_async_copy(*pair, sem.at[k]) for k, pair in enumerate(pairs)]
    for copy in copies:
        copy.start()
    return copies


def cell_rates(cond, diffusivity, width, depth):
    lane = lax.broadcasted_iota(jnp.int32, (depth, width), 1)
    same_depth = lax.rem(lane, depth) == lax.broadcasted_iota(jnp.int32, (depth, width), 0)
    species = width // depth
    lane = lax.broadcasted_iota(jnp.int32, (species, width), 1)
    same_species = lax.div(lane, depth) == lax.broadcasted_iota(jnp.int32, (species, width), 0)
    highest = lax.Precision.HIGHEST
    spread = jnp.dot(
        (1.0 / cond).reshape(-1, depth),
        same_depth.astype(jnp.float32),
        precision=highest,
        preferred_element_type=jnp.float32,
    )
    scale = jnp.dot(
        jnp.broadcast_to(1.0 / diffusivity, (CELLS, species)),
        same_species.astype(jnp.float32),
        precision=highest,
        preferred_element_type=jnp.float32,
    )
    tiles = spread.reshape(CELLS, CELLS, width)
    return [tiles[cell] * scale for cell in range(CELLS)]


def factors(rates):
    one = jnp.ones_like(rates[0])
    zero = jnp.zeros_like(one)

    def shoot(value, step, order):
        values = {}
        for cell in order:
            values[cell] = value
            step = step + rates[cell] * value
            value = value + step
        return values, value, step

    flat, flat_out, flat_step = shoot(one, zero, range(CELLS))
    slope, slope_out, slope_step = shoot(zero, one, range(CELLS))
    right, _, _ = shoot(one, one, reversed(range(CELLS)))
    inverse = 1.0 / (flat_out + slope_out)
    to_last = [(flat[k] + slope[k]) * inverse for k in range(CELLS)]
    to_first = [right[k] * inverse for k in range(CELLS)]
    transfer = (flat_step, slope_step, flat[CELLS - 1], slope[CELLS - 1])
    return to_first, to_last, transfer


def sweep_factors(to_first, to_last):
    ratio = to_last[0] * 0.0
    forward = [to_last[k] / to_last[k + 1] for k in range(CELLS - 1)] + [ratio]
    backward = [ratio] + [to_first[k] / to_first[k - 1] for k in range(1, CELLS)]
    scale = 1.0 / to_first[CELLS - 1]
    gains = [to_first[k] * to_last[k] * scale for k in range(CELLS)]
    return forward, backward, gains


def local_solution(sources, forward, backward, gains):
    before, after = [None] * CELLS, [None] * CELLS
    running = sources[0] * 0.0
    for k in range(CELLS):
        before[k] = sources[k] + running
        running = forward[k] * before[k]
    running = sources[0] * 0.0
    for k in reversed(range(CELLS)):
        after[k] = running
        running = backward[k] * (sources[k] + running)
    return [(before[k] + after[k]) * gains[k] for k in range(CELLS)]


def total(weights, sources):
    terms = [weight * source for weight, source in zip(weights, sources, strict=True)]
    while len(terms) > 1:
        terms = [a + b for a, b in zip(terms[::2], terms[1::2], strict=True)]
    return terms[0]


def put_rows(send_ref, rows):
    for row, value in enumerate(rows):
        for tile in range(value.shape[1] // LANES):
            send_ref[pl.ds(tile * ROWS + row, CELLS, stride=CELLS * 4), :] = value[
                :, tile * LANES : (tile + 1) * LANES
            ]


def get_ends(back_ref):
    return [
        jnp.concatenate(
            [back_ref[pl.ds(tile * 2 + side, CELLS, stride=CELLS), :] for tile in range(4)], axis=1
        )
        for side in range(2)
    ]


def start_kernel(
    depth, cot_from, cond_from, diffusivity_from, send_ref, cot_ref, cond_ref, diffusivity_ref, sem
):
    width = cot_ref.shape[2]
    copies = begin(
        [(cond_from, cond_ref), (diffusivity_from, diffusivity_ref), (cot_from, cot_ref)], sem
    )
    copies[0].wait()
    copies[1].wait()
    cond = jnp.swapaxes(cond_ref[...], 0, 1)
    rates = cell_rates(cond, diffusivity_ref[...], width, depth)
    to_first, to_last, transfer = factors(rates)
    copies[2].wait()
    lines = jnp.swapaxes(cot_ref[...], 0, 1)
    sources = [lines[cell] for cell in range(CELLS)]
    blank = jnp.zeros_like(rates[0])
    put_rows(
        send_ref,
        [total(to_first, sources), total(to_last, sources), *transfer, blank, blank],
    )


def solve_kernel(blocks, tiles, got_ref, out_ref, *scratch):
    value_l, step_l, value_r, step_r, ratio_l, add_l, ratio_r, add_r, sum_l, sum_r = scratch
    one = jnp.ones((1, LANES), jnp.float32)

    def pick(block, tile, row):
        return got_ref[pl.ds((block * tiles + tile) * ROWS + row, 1), :]

    def whole(tile, row):
        return got_ref[pl.ds(tile * ROWS + row, blocks, stride=ROWS * tiles), :]

    for tile in range(tiles):
        left, left_step, right, right_step = one, one, one, one
        for block in range(blocks):
            mirror = blocks - 1 - block
            value_l[tile, pl.ds(block, 1), :] = left
            step_l[tile, pl.ds(block, 1), :] = left_step
            value_r[tile, pl.ds(mirror + 1, 1), :] = right
            step_r[tile, pl.ds(mirror + 1, 1), :] = right_step
            c, d, e, f = (pick(block, tile, row) for row in range(2, 6))
            kept = e * left + f * left_step
            left_step = c * left + d * left_step
            left = kept + left_step
            c, d, e, f = (pick(mirror, tile, row) for row in range(2, 6))
            kept = d * right + f * right_step
            right_step = c * right + e * right_step
            right = kept + right_step
        value_l[tile, pl.ds(blocks, 1), :] = left
        step_l[tile, pl.ds(blocks, 1), :] = left_step
        value_r[tile, pl.ds(0, 1), :] = right
        step_r[tile, pl.ds(0, 1), :] = right_step
    for tile in range(tiles):
        near = pl.ds(0, blocks)
        far = pl.ds(1, blocks)
        first, last = whole(tile, 0), whole(tile, 1)
        inverse = 1.0 / value_l[tile, far, :]
        at = value_l[tile, near, :]
        ratio_l[tile] = at * inverse
        add_l[tile] = last + (at - step_l[tile, near, :]) * inverse * first
        inverse = 1.0 / value_r[tile, near, :]
        at = value_r[tile, far, :]
        ratio_r[tile] = at * inverse
        add_r[tile] = first + (at - step_r[tile, far, :]) * inverse * last
    for tile in range(tiles):
        left = jnp.zeros_like(one)
        right = jnp.zeros_like(one)
        for block in range(blocks):
            mirror = blocks - 1 - block
            sum_l[tile, pl.ds(block, 1), :] = left
            sum_r[tile, pl.ds(mirror + 1, 1), :] = right
            here, there = pl.ds(block, 1), pl.ds(mirror, 1)
            left = ratio_l[tile, here, :] * left + add_l[tile, here, :]
            right = ratio_r[tile, there, :] * right + add_r[tile, there, :]
        sum_l[tile, pl.ds(blocks, 1), :] = left
        sum_r[tile, pl.ds(0, 1), :] = right
    for tile in range(tiles):
        for side in range(2):
            rows = pl.ds(side, blocks)
            gap_l = step_l[tile, rows, :] / value_l[tile, rows, :]
            gap_r = step_r[tile, rows, :] / value_r[tile, rows, :]
            inverse = 1.0 / (gap_l + gap_r * (1.0 - gap_l))
            left, right = sum_l[tile, rows, :], sum_r[tile, rows, :]
            if side == 0:
                ends = (left + (1.0 - gap_l) * right) * inverse
            else:
                ends = (right + (1.0 - gap_r) * left) * inverse
            out_ref[pl.ds(tile * 2 + side, blocks, stride=2 * tiles), :] = ends


def to_species(cells, turn_ref, depth):
    rows = cells.shape[0]
    turn_ref[...] = jnp.concatenate([cells, cells], axis=0).T
    species = cells.shape[1] // depth
    low = lax.broadcasted_iota(jnp.int32, (species, 2 * rows), 1) < rows
    pairs = []
    for pair in range(depth // 2):
        even = turn_ref[pl.ds(2 * pair, species, stride=depth), :]
        odd = turn_ref[pl.ds(2 * pair + 1, species, stride=depth), :]
        pairs.append(jnp.where(low, even, odd))
    return pairs


def from_species(pairs, turn_ref, depth):
    species, columns = pairs[0].shape
    for pair, tile in enumerate(pairs):
        turn_ref[pl.ds(2 * pair, species, stride=depth), :] = tile
        turn_ref[pl.ds(2 * pair + 1, species, stride=depth), :] = pltpu.roll(
            tile, columns // 2, 1
        )
    return turn_ref[...].T[: columns // 2]


def halves(value):
    high = value.astype(jnp.bfloat16)
    return high, (value - high.astype(jnp.float32)).astype(jnp.bfloat16)


def counts(pair_ref, species):
    ids = lax.broadcasted_iota(jnp.int32, (pair_ref.shape[0], species), 1)
    return (pair_ref[:, 0:1] == ids).astype(jnp.float32) + (pair_ref[:, 1:2] == ids).astype(
        jnp.float32
    )


def counts(pair_ref, species):
    ids = lax.broadcasted_iota(jnp.int32, (species, pair_ref.shape[1]), 0)
    return (pair_ref[0:1, :] == ids).astype(jnp.float32) + (pair_ref[1:2, :] == ids).astype(
        jnp.float32
    )


def prepare_kernel(
    depth, cot_from, conc_from, cond_from, diffusivity_from, rate_from, reactants_from,
    products_from, jacobian_to, inverse_ref, local_y_ref, ends_y_ref, ends_x_ref, sweep_x_ref,
    transfer_ref, cot_ref, conc_ref, cond_ref, diffusivity_ref, rate_ref, reactants_ref,
    products_ref, turn_ref, rates_ref, pairs_ref, jacobian_ref, in_sem, sem,
):
    inputs = begin(
        [
            (reactants_from, reactants_ref),
            (products_from, products_ref),
            (rate_from, rate_ref),
            (conc_from, conc_ref),
            (cond_from, cond_ref),
            (diffusivity_from, diffusivity_ref),
            (cot_from, cot_ref),
        ],
        in_sem,
    )
    for copy in inputs:
        copy.wait()
    rows_x, rows_y, width = conc_ref.shape
    species = width // depth
    used = counts(reactants_ref, species)
    net = counts(products_ref, species) - used
    for s in range(species):
        product = (net[s : s + 1, :] * used).astype(jnp.bfloat16)
        rows = pl.ds(s * species, species)
        pairs_ref[rows, : used.shape[1]] = product
        pairs_ref[rows, used.shape[1] :] = product
    twice = jnp.concatenate([used, used], axis=0).T.astype(jnp.bfloat16)
    constant = jnp.broadcast_to(rate_ref[...], (LANES, rate_ref.shape[1])).T
    pairs = to_species(conc_ref[...].reshape(rows_x * rows_y, width), turn_ref, depth)
    for pair, conc in enumerate(pairs):
        columns = pl.ds(pair * conc.shape[1], conc.shape[1])
        inverse_ref[:, columns] = 1.0 / conc
        stacked = jnp.concatenate(halves(jnp.log(conc)), axis=0)
        exponent = jnp.dot(twice, stacked, preferred_element_type=jnp.float32)
        rates_ref[:, columns] = jnp.concatenate(halves(constant * jnp.exp(exponent)), axis=0)
    wide = 2 * LANES
    copies = []
    for chunk in range(rates_ref.shape[1] // wide):
        columns = pl.ds(chunk * wide, wide)
        block = jnp.dot(pairs_ref[...], rates_ref[:, columns], preferred_element_type=jnp.float32)
        for part in range(2):
            jacobian_ref[2 * chunk + part] = block[:, part * LANES : (part + 1) * LANES]
        tiles = pl.ds(2 * chunk, 2)
        copies.append(
            pltpu.make_async_copy(jacobian_ref.at[tiles], jacobian_to.at[tiles], sem.at[chunk])
        )
        copies[-1].start()

    cond = cond_ref[...]
    rates = cell_rates(cond, diffusivity_ref[...], width, depth)
    to_first, to_last, transfer = factors(rates)
    forward, backward, gains = sweep_factors(to_first, to_last)
    for k in range(CELLS):
        ends_x_ref[0, k] = to_first[k]
        ends_x_ref[1, k] = to_last[k]
        sweep_x_ref[0, k] = forward[k]
        sweep_x_ref[1, k] = backward[k]
        sweep_x_ref[2, k] = gains[k] * rates[k]
        sweep_x_ref[3, k] = to_first[k] * rates[k]
        sweep_x_ref[4, k] = to_last[k] * rates[k]
    for k in range(4):
        transfer_ref[k] = transfer[k]
    rates = cell_rates(jnp.swapaxes(cond, 0, 1), diffusivity_ref[...], width, depth)
    to_first, to_last, _ = factors(rates)
    lines = jnp.swapaxes(cot_ref[...], 0, 1)
    local = local_solution(
        [lines[k] for k in range(CELLS)], *sweep_factors(to_first, to_last)
    )
    for k in range(CELLS):
        local_y_ref[k] = local[k] * rates[k]
        ends_y_ref[0, k] = to_first[k] * rates[k]
        ends_y_ref[1, k] = to_last[k] * rates[k]
    for copy in copies:
        copy.wait()


def chemistry(field, columns, jacobian_ref, inverse, vector_ref):
    species = field.shape[0]

    def transposed(vector):
        vector_ref[:, columns] = vector
        sums = [None] * 4
        for s in range(species):
            row = jnp.broadcast_to(vector_ref[pl.ds(s, 1), columns], vector.shape)
            term = row * jacobian_ref[pl.ds(s * species, species), :]
            sums[s % 4] = term if sums[s % 4] is None else sums[s % 4] + term
        return ((sums[0] + sums[1]) + (sums[2] + sums[3])) * inverse

    third = field + transposed(field) * (1.0 / 3.0)
    second = field + transposed(third) * 0.5
    return field + transposed(second)


def middle_kernel(
    depth, ends_ref, local_ref, ends_y_ref, jacobian_from, inverse_ref, ends_x_ref, transfer_ref,
    send_ref, sources_ref, turn_ref, vector_ref, jacobian_ref, sem,
):
    width = local_ref.shape[2]
    tiles = range(jacobian_ref.shape[0])
    copies = begin([(jacobian_from.at[tile], jacobian_ref.at[tile]) for tile in tiles], sem)
    left, right = get_ends(ends_ref)
    solved = jnp.stack(
        [
            local_ref[k] + ends_y_ref[0, k] * left + ends_y_ref[1, k] * right
            for k in range(CELLS)
        ],
        axis=0,
    )
    solved = jnp.swapaxes(solved, 0, 1).reshape(CELLS * CELLS, width)
    pairs = to_species(solved, turn_ref, depth)
    done = []
    for pair, field in enumerate(pairs):
        columns = pl.ds(pair * field.shape[1], field.shape[1])
        copies[pair].wait()
        jacobian = jacobian_ref.at[pair]
        done.append(chemistry(field, columns, jacobian, inverse_ref[:, columns], vector_ref))
    changed = from_species(done, turn_ref, depth).reshape(CELLS, CELLS, width)
    sources_ref[...] = changed
    sources = [changed[k] for k in range(CELLS)]
    blank = jnp.zeros_like(left)
    put_rows(
        send_ref,
        [
            total([ends_x_ref[0, k] for k in range(CELLS)], sources),
            total([ends_x_ref[1, k] for k in range(CELLS)], sources),
            *(transfer_ref[k] for k in range(4)),
            blank,
            blank,
        ],
    )


def finish_kernel(ends_ref, sources_ref, sweep_ref, out_ref):
    local = local_solution(
        [sources_ref[k] for k in range(CELLS)],
        *([sweep_ref[part, k] for k in range(CELLS)] for part in range(3)),
    )
    left, right = get_ends(ends_ref)
    for k in range(CELLS):
        out_ref[k] = local[k] + sweep_ref[3, k] * left + sweep_ref[4, k] * right


def exchange(rows, axis):
    members = lax.axis_size(axis)
    blocks = rows.reshape(members, rows.shape[0] // members, LANES)
    return lax.all_to_all(blocks, axis, 0, 0, tiled=True).reshape(rows.shape)


def solve_lines(send, axis):
    blocks = lax.axis_size(axis)
    tiles = send.shape[0] // (blocks * ROWS)
    states = pltpu.VMEM((tiles, blocks + CELLS, LANES), jnp.float32)
    terms = pltpu.VMEM((tiles, blocks, LANES), jnp.float32)
    ends = call(
        functools.partial(solve_kernel, blocks, tiles),
        struct(2 * blocks * tiles, LANES),
        [states] * 4 + [terms] * 4 + [states] * 2,
    )(exchange(send, axis))
    return exchange(ends, axis)


def on_device(
    cotangent, concentration, conductance, diffusivity, rate_constant, reactants, products
):
    rows_x, rows_y, width = cotangent.shape
    depth = conductance.shape[2]
    species = diffusivity.shape[0]
    reactions = rate_constant.shape[0]
    columns = rows_x * rows_y * depth
    diffusivity = diffusivity[None, :]
    turn = pltpu.VMEM((width, 2 * rows_x * rows_y), jnp.float32)
    block = struct(CELLS, CELLS, width)
    send = struct(CELLS * (width // LANES) * ROWS, LANES)

    send_y = call(
        functools.partial(start_kernel, depth),
        send,
        [
            pltpu.VMEM(cotangent.shape, jnp.float32),
            pltpu.VMEM(conductance.shape, jnp.float32),
            pltpu.VMEM(diffusivity.shape, jnp.float32),
            pltpu.SemaphoreType.DMA((3,)),
        ],
        far_in=(0, 1, 2),
    )(cotangent, conductance, diffusivity)
    jacobian, inverse, local_y, ends_y, ends_x, sweep_x, transfer = call(
        functools.partial(prepare_kernel, depth),
        [
            pltpu.HBM((columns // LANES, species * species, LANES), jnp.float32),
            struct(species, columns),
            block,
            struct(2, CELLS, CELLS, width),
            struct(2, CELLS, CELLS, width),
            struct(5, CELLS, CELLS, width),
            struct(4, CELLS, width),
        ],
        [
            pltpu.VMEM(cotangent.shape, jnp.float32),
            pltpu.VMEM(concentration.shape, jnp.float32),
            pltpu.VMEM(conductance.shape, jnp.float32),
            pltpu.VMEM(diffusivity.shape, jnp.float32),
            pltpu.VMEM((1, reactions), jnp.float32),
            pltpu.VMEM((2, reactions), jnp.int32),
            pltpu.VMEM((2, reactions), jnp.int32),
            turn,
            pltpu.VMEM((2 * reactions, columns), jnp.bfloat16),
            pltpu.VMEM((species * species, 2 * reactions), jnp.bfloat16),
            pltpu.VMEM((columns // LANES, species * species, LANES), jnp.float32),
            pltpu.SemaphoreType.DMA((7,)),
            pltpu.SemaphoreType.DMA((columns // (2 * LANES),)),
        ],
        far_in=tuple(range(7)),
        far_out=(0,),
    )(
        cotangent,
        concentration,
        conductance,
        diffusivity,
        rate_constant[None, :],
        reactants.T,
        products.T,
    )
    got_y = solve_lines(send_y, "gy")
    send_x, sources = call(
        functools.partial(middle_kernel, depth),
        [send, block],
        [
            turn,
            pltpu.VMEM((species, columns), jnp.float32),
            pltpu.VMEM((columns // LANES, species * species, LANES), jnp.float32),
            pltpu.SemaphoreType.DMA((columns // LANES,)),
        ],
        far_in=(3,),
    )(got_y, local_y, ends_y, jacobian, inverse, ends_x, transfer)
    got_x = solve_lines(send_x, "gx")
    return call(finish_kernel, block)(got_x, sources, sweep_x)


def solution(mesh):
    placed = (P("gx", "gy", None), P("gx", "gy", None), P("gx", "gy", None), P(), P(), P(), P())
    return jax.shard_map(
        on_device, mesh=mesh, in_specs=placed, out_specs=P("gx", "gy", None), check_vma=False
    )
```

```python
import functools

import jax
import jax.numpy as jnp
from jax import lax
from jax.experimental import pallas as pl
from jax.experimental.pallas import tpu as pltpu
from jax.sharding import PartitionSpec as P


CELLS = 8
LANES = 128
ROWS = 4
NEAR = 3
LIMIT = 16 << 20


def call(kernel, out_shape, scratch_shapes=(), far_in=(), far_out=()):
    near = pl.BlockSpec(memory_space=pltpu.VMEM)
    far = pl.BlockSpec(memory_space=pltpu.HBM)

    def run(*operands):
        operands = [
            pltpu.with_memory_space_constraint(x, pltpu.HBM) if k in far_in else x
            for k, x in enumerate(operands)
        ]
        outs = near
        if isinstance(out_shape, list):
            outs = [far if k in far_out else near for k in range(len(out_shape))]
        return pl.pallas_call(
            kernel,
            out_shape=out_shape,
            in_specs=[far if k in far_in else near for k in range(len(operands))],
            out_specs=outs,
            scratch_shapes=list(scratch_shapes),
            compiler_params=pltpu.CompilerParams(vmem_limit_bytes=LIMIT),
        )(*operands)

    return run


def struct(*shape):
    return jax.ShapeDtypeStruct(shape, jnp.float32)


def begin(pairs, sem):
    copies = [pltpu.make_async_copy(*pair, sem.at[k]) for k, pair in enumerate(pairs)]
    for copy in copies:
        copy.start()
    return copies


def species_scale(diffusivity, width, depth):
    species = width // depth
    lane = lax.broadcasted_iota(jnp.int32, (species, width), 1)
    same = lax.div(lane, depth) == lax.broadcasted_iota(jnp.int32, (species, width), 0)
    return jnp.dot(
        jnp.broadcast_to(1.0 / diffusivity, (CELLS, species)),
        same.astype(jnp.float32),
        precision=lax.Precision.HIGHEST,
        preferred_element_type=jnp.float32,
    )


def cell_rates(cond, scale, depth):
    width = scale.shape[1]
    lane = lax.broadcasted_iota(jnp.int32, (depth, width), 1)
    same = lax.rem(lane, depth) == lax.broadcasted_iota(jnp.int32, (depth, width), 0)
    spread = jnp.dot(
        (1.0 / cond).reshape(-1, depth),
        same.astype(jnp.float32),
        precision=lax.Precision.HIGHEST,
        preferred_element_type=jnp.float32,
    )
    tiles = spread.reshape(CELLS, CELLS, width)
    return [tiles[cell] * scale for cell in range(CELLS)]


def shoot(rates, value, step, order):
    values = [None] * CELLS
    for cell in order:
        values[cell] = value
        step = step + rates[cell] * value
        value = value + step
    return values, value, step


def factors(rates):
    one = jnp.ones_like(rates[0])
    left, out, _ = shoot(rates, one, one, range(CELLS))
    right, _, _ = shoot(rates, one, one, reversed(range(CELLS)))
    inverse = 1.0 / out
    return [value * inverse for value in right], [value * inverse for value in left]


def sweep_factors(to_first, to_last):
    ratio = to_last[0] * 0.0
    forward = [to_last[k] / to_last[k + 1] for k in range(CELLS - 1)] + [ratio]
    backward = [ratio] + [to_first[k] / to_first[k - 1] for k in range(1, CELLS)]
    scale = 1.0 / to_first[CELLS - 1]
    gains = [to_first[k] * to_last[k] * scale for k in range(CELLS)]
    return forward, backward, gains


def local_solution(sources, forward, backward, gains):
    before, after = [None] * CELLS, [None] * CELLS
    running = sources[0] * 0.0
    for k in range(CELLS):
        before[k] = sources[k] + running
        running = forward[k] * before[k]
    running = sources[0] * 0.0
    for k in reversed(range(CELLS)):
        after[k] = running
        running = backward[k] * (sources[k] + running)
    return [(before[k] + after[k]) * gains[k] for k in range(CELLS)]


def total(weights, sources):
    terms = [weight * source for weight, source in zip(weights, sources, strict=True)]
    while len(terms) > 1:
        terms = [a + b for a, b in zip(terms[::2], terms[1::2], strict=True)]
    return terms[0]


def put_rows(send_ref, rows):
    for row, value in enumerate(rows):
        for tile in range(4):
            part = value
            if value.shape[1] > LANES:
                part = value[:, tile * LANES : (tile + 1) * LANES]
            send_ref[pl.ds(tile * ROWS + row, CELLS, stride=4 * ROWS), :] = part


def pack(cond):
    return jnp.concatenate([cond[cell] for cell in range(CELLS)], axis=1)


def get_ends(back_ref):
    return [
        jnp.concatenate(
            [back_ref[pl.ds(tile * 2 + side, CELLS, stride=CELLS), :] for tile in range(4)], axis=1
        )
        for side in range(2)
    ]


def start_kernel(
    depth, cot_from, cond_from, diffusivity_from, send_ref, scale_ref, cot_ref, cond_ref,
    diffusivity_ref, sem,
):
    width = cot_ref.shape[2]
    copies = begin(
        [(cond_from, cond_ref), (diffusivity_from, diffusivity_ref), (cot_from, cot_ref)], sem
    )
    copies[0].wait()
    copies[1].wait()
    cond = jnp.swapaxes(cond_ref[...], 0, 1)
    scale = species_scale(diffusivity_ref[...], width, depth)
    to_first, to_last = factors(cell_rates(cond, scale, depth))
    packed = pack(cond)
    for tile in range(4):
        scale_ref[pl.ds(tile, 1), :] = scale[0:1, tile * LANES : (tile + 1) * LANES]
    copies[2].wait()
    lines = jnp.swapaxes(cot_ref[...], 0, 1)
    sources = [lines[cell] for cell in range(CELLS)]
    put_rows(
        send_ref,
        [total(to_first, sources), total(to_last, sources), packed, jnp.zeros_like(packed)],
    )


def solve_kernel(depth, axis, blocks, tiles, got_ref, scale_ref, out_ref, *scratch):
    value_l, step_l, value_r, step_r, ratio_l, add_l, ratio_r, add_r, sum_l, sum_r = scratch[:10]
    moves = scratch[10:]
    me = lax.axis_index(axis)
    one = jnp.ones((1, LANES), jnp.float32)

    def whole(tile, row):
        return got_ref[pl.ds(tile * ROWS + row, blocks, stride=ROWS * tiles), :]

    for tile in range(tiles):
        scale = scale_ref[pl.ds(lax.rem(me * tiles + tile, 4), 1), :]
        inverse = 1.0 / whole(tile, 2)
        lane = lax.rem(lax.broadcasted_iota(jnp.int32, inverse.shape, 1), depth)
        rates = [
            jnp.take_along_axis(
                inverse, lane + cell * depth, axis=1, mode="promise_in_bounds"
            )
            * scale
            for cell in range(CELLS)
        ]
        ones = jnp.ones_like(inverse)
        flat, _, flat_step = shoot(rates, ones, ones * 0.0, range(CELLS))
        slope, _, slope_step = shoot(rates, ones * 0.0, ones, range(CELLS))
        last = CELLS - 1
        for move, value in zip(moves, (flat_step, slope_step, flat[last], slope[last]), strict=True):
            move[tile] = value
    for tile in range(tiles):
        left, left_step, right, right_step = one, one, one, one
        for block in range(blocks):
            mirror = blocks - 1 - block
            value_l[tile, pl.ds(block, 1), :] = left
            step_l[tile, pl.ds(block, 1), :] = left_step
            value_r[tile, pl.ds(mirror + 1, 1), :] = right
            step_r[tile, pl.ds(mirror + 1, 1), :] = right_step
            c, d, e, f = (move[tile, pl.ds(block, 1), :] for move in moves)
            kept = e * left + f * left_step
            left_step = c * left + d * left_step
            left = kept + left_step
            c, d, e, f = (move[tile, pl.ds(mirror, 1), :] for move in moves)
            kept = d * right + f * right_step
            right_step = c * right + e * right_step
            right = kept + right_step
        value_l[tile, pl.ds(blocks, 1), :] = left
        step_l[tile, pl.ds(blocks, 1), :] = left_step
        value_r[tile, pl.ds(0, 1), :] = right
        step_r[tile, pl.ds(0, 1), :] = right_step
    for tile in range(tiles):
        near = pl.ds(0, blocks)
        far = pl.ds(1, blocks)
        first, last = whole(tile, 0), whole(tile, 1)
        inverse = 1.0 / value_l[tile, far, :]
        at = value_l[tile, near, :]
        ratio_l[tile] = at * inverse
        add_l[tile] = last + (at - step_l[tile, near, :]) * inverse * first
        inverse = 1.0 / value_r[tile, near, :]
        at = value_r[tile, far, :]
        ratio_r[tile] = at * inverse
        add_r[tile] = first + (at - step_r[tile, far, :]) * inverse * last
    for tile in range(tiles):
        left = jnp.zeros_like(one)
        right = jnp.zeros_like(one)
        for block in range(blocks):
            mirror = blocks - 1 - block
            sum_l[tile, pl.ds(block, 1), :] = left
            sum_r[tile, pl.ds(mirror + 1, 1), :] = right
            here, there = pl.ds(block, 1), pl.ds(mirror, 1)
            left = ratio_l[tile, here, :] * left + add_l[tile, here, :]
            right = ratio_r[tile, there, :] * right + add_r[tile, there, :]
        sum_l[tile, pl.ds(blocks, 1), :] = left
        sum_r[tile, pl.ds(0, 1), :] = right
    for tile in range(tiles):
        for side in range(2):
            rows = pl.ds(side, blocks)
            gap_l = step_l[tile, rows, :] / value_l[tile, rows, :]
            gap_r = step_r[tile, rows, :] / value_r[tile, rows, :]
            inverse = 1.0 / (gap_l + gap_r * (1.0 - gap_l))
            left, right = sum_l[tile, rows, :], sum_r[tile, rows, :]
            if side == 0:
                ends = (left + (1.0 - gap_l) * right) * inverse
            else:
                ends = (right + (1.0 - gap_r) * left) * inverse
            out_ref[pl.ds(tile * 2 + side, blocks, stride=2 * tiles), :] = ends


def to_species(cells, turn_ref, depth):
    rows = cells.shape[0]
    turn_ref[...] = jnp.concatenate([cells, cells], axis=0).T
    species = cells.shape[1] // depth
    low = lax.broadcasted_iota(jnp.int32, (species, 2 * rows), 1) < rows
    pairs = []
    for pair in range(depth // 2):
        even = turn_ref[pl.ds(2 * pair, species, stride=depth), :]
        odd = turn_ref[pl.ds(2 * pair + 1, species, stride=depth), :]
        pairs.append(jnp.where(low, even, odd))
    return pairs


def from_species(pairs, turn_ref, depth):
    species, columns = pairs[0].shape
    for pair, tile in enumerate(pairs):
        turn_ref[pl.ds(2 * pair, species, stride=depth), :] = tile
        turn_ref[pl.ds(2 * pair + 1, species, stride=depth), :] = pltpu.roll(
            tile, columns // 2, 1
        )
    return turn_ref[...].T[: columns // 2]


def halves(value):
    high = value.astype(jnp.bfloat16)
    return high, (value - high.astype(jnp.float32)).astype(jnp.bfloat16)


def counts(pair_ref, species):
    ids = lax.broadcasted_iota(jnp.int32, (pair_ref.shape[0], species), 1)
    return (pair_ref[:, 0:1] == ids).astype(jnp.float32) + (pair_ref[:, 1:2] == ids).astype(
        jnp.float32
    )


def counts(pair_ref, species):
    ids = lax.broadcasted_iota(jnp.int32, (species, pair_ref.shape[1]), 0)
    return (pair_ref[0:1, :] == ids).astype(jnp.float32) + (pair_ref[1:2, :] == ids).astype(
        jnp.float32
    )


def prepare_kernel(
    depth, cot_from, conc_from, cond_from, diffusivity_from, rate_from, reactants_from,
    products_from, jacobian_to, jacobian_near_ref, inverse_ref, local_y_ref, ends_y_ref,
    ends_x_ref, sweep_x_ref, packed_x_ref, cot_ref, conc_ref, cond_ref, diffusivity_ref, rate_ref, reactants_ref,
    products_ref, turn_ref, rates_ref, pairs_ref, jacobian_ref, in_sem, sem,
):
    inputs = begin(
        [
            (reactants_from, reactants_ref),
            (products_from, products_ref),
            (rate_from, rate_ref),
            (conc_from, conc_ref),
            (cond_from, cond_ref),
            (diffusivity_from, diffusivity_ref),
            (cot_from, cot_ref),
        ],
        in_sem,
    )
    for copy in inputs:
        copy.wait()
    rows_x, rows_y, width = conc_ref.shape
    species = width // depth
    used = counts(reactants_ref, species)
    net = counts(products_ref, species) - used
    for s in range(species):
        product = (net[s : s + 1, :] * used).astype(jnp.bfloat16)
        rows = pl.ds(s * species, species)
        pairs_ref[rows, : used.shape[1]] = product
        pairs_ref[rows, used.shape[1] :] = product
    twice = jnp.concatenate([used, used], axis=0).T.astype(jnp.bfloat16)
    constant = jnp.broadcast_to(rate_ref[...], (LANES, rate_ref.shape[1])).T
    pairs = to_species(conc_ref[...].reshape(rows_x * rows_y, width), turn_ref, depth)
    for pair, conc in enumerate(pairs):
        columns = pl.ds(pair * conc.shape[1], conc.shape[1])
        inverse_ref[:, columns] = 1.0 / conc
        stacked = jnp.concatenate(halves(jnp.log(conc)), axis=0)
        exponent = jnp.dot(twice, stacked, preferred_element_type=jnp.float32)
        rates_ref[:, columns] = jnp.concatenate(halves(constant * jnp.exp(exponent)), axis=0)
    wide = 2 * LANES
    copies = []
    for chunk in range(rates_ref.shape[1] // wide):
        columns = pl.ds(chunk * wide, wide)
        block = jnp.dot(pairs_ref[...], rates_ref[:, columns], preferred_element_type=jnp.float32)
        for part in range(2):
            tile = 2 * chunk + part - jacobian_ref.shape[0]
            value = block[:, part * LANES : (part + 1) * LANES]
            if tile >= 0:
                jacobian_near_ref[tile] = value
                continue
            tile += jacobian_ref.shape[0]
            jacobian_ref[tile] = value
            copies.append(
                pltpu.make_async_copy(jacobian_ref.at[tile], jacobian_to.at[tile], sem.at[tile])
            )
            copies[-1].start()

    cond = cond_ref[...]
    scale = species_scale(diffusivity_ref[...], width, depth)
    packed_x_ref[...] = pack(cond)
    rates = cell_rates(cond, scale, depth)
    to_first, to_last = factors(rates)
    forward, backward, gains = sweep_factors(to_first, to_last)
    for k in range(CELLS):
        ends_x_ref[0, k] = to_first[k]
        ends_x_ref[1, k] = to_last[k]
        sweep_x_ref[0, k] = forward[k]
        sweep_x_ref[1, k] = backward[k]
        sweep_x_ref[2, k] = gains[k] * rates[k]
        sweep_x_ref[3, k] = to_first[k] * rates[k]
        sweep_x_ref[4, k] = to_last[k] * rates[k]
    rates = cell_rates(jnp.swapaxes(cond, 0, 1), scale, depth)
    to_first, to_last = factors(rates)
    lines = jnp.swapaxes(cot_ref[...], 0, 1)
    local = local_solution([lines[k] for k in range(CELLS)], *sweep_factors(to_first, to_last))
    for k in range(CELLS):
        local_y_ref[k] = local[k] * rates[k]
        ends_y_ref[0, k] = to_first[k] * rates[k]
        ends_y_ref[1, k] = to_last[k] * rates[k]
    for copy in copies:
        copy.wait()


def chemistry(field, columns, jacobian_ref, inverse, vector_ref):
    species = field.shape[0]

    def transposed(vector):
        vector_ref[:, columns] = vector
        sums = [None] * 4
        for s in range(species):
            row = jnp.broadcast_to(vector_ref[pl.ds(s, 1), columns], vector.shape)
            term = row * jacobian_ref[pl.ds(s * species, species), :]
            sums[s % 4] = term if sums[s % 4] is None else sums[s % 4] + term
        return ((sums[0] + sums[1]) + (sums[2] + sums[3])) * inverse

    third = field + transposed(field) * (1.0 / 3.0)
    second = field + transposed(third) * 0.5
    return field + transposed(second)


def middle_kernel(
    depth, ends_ref, local_ref, ends_y_ref, jacobian_from, jacobian_near_ref, inverse_ref,
    ends_x_ref, packed_x_ref, send_ref, sources_ref, turn_ref, vector_ref, jacobian_ref, sem,
):
    width = local_ref.shape[2]
    far = jacobian_ref.shape[0]
    copies = begin(
        [(jacobian_from.at[tile], jacobian_ref.at[tile]) for tile in range(far)], sem
    )
    left, right = get_ends(ends_ref)
    solved = jnp.stack(
        [
            local_ref[k] + ends_y_ref[0, k] * left + ends_y_ref[1, k] * right
            for k in range(CELLS)
        ],
        axis=0,
    )
    solved = jnp.swapaxes(solved, 0, 1).reshape(CELLS * CELLS, width)
    pairs = to_species(solved, turn_ref, depth)
    done = [None] * len(pairs)
    for pair in [*range(far, len(pairs)), *range(far)]:
        field = pairs[pair]
        columns = pl.ds(pair * field.shape[1], field.shape[1])
        if pair < far:
            copies[pair].wait()
            jacobian = jacobian_ref.at[pair]
        else:
            jacobian = jacobian_near_ref.at[pair - far]
        done[pair] = chemistry(field, columns, jacobian, inverse_ref[:, columns], vector_ref)
    changed = from_species(done, turn_ref, depth).reshape(CELLS, CELLS, width)
    sources_ref[...] = changed
    sources = [changed[k] for k in range(CELLS)]
    packed = packed_x_ref[...]
    put_rows(
        send_ref,
        [
            total([ends_x_ref[0, k] for k in range(CELLS)], sources),
            total([ends_x_ref[1, k] for k in range(CELLS)], sources),
            packed,
            jnp.zeros_like(packed),
        ],
    )


def finish_kernel(ends_ref, sources_ref, sweep_ref, out_ref):
    local = local_solution(
        [sources_ref[k] for k in range(CELLS)],
        *([sweep_ref[part, k] for k in range(CELLS)] for part in range(3)),
    )
    left, right = get_ends(ends_ref)
    for k in range(CELLS):
        out_ref[k] = local[k] + sweep_ref[3, k] * left + sweep_ref[4, k] * right


def exchange(rows, axis):
    members = lax.axis_size(axis)
    blocks = rows.reshape(members, rows.shape[0] // members, LANES)
    return lax.all_to_all(blocks, axis, 0, 0, tiled=True).reshape(rows.shape)


def solve_lines(send, scale, axis, depth):
    blocks = lax.axis_size(axis)
    tiles = send.shape[0] // (blocks * ROWS)
    states = pltpu.VMEM((tiles, blocks + CELLS, LANES), jnp.float32)
    terms = pltpu.VMEM((tiles, blocks, LANES), jnp.float32)
    ends = call(
        functools.partial(solve_kernel, depth, axis, blocks, tiles),
        struct(2 * blocks * tiles, LANES),
        [states] * 4 + [terms] * 4 + [states] * 2 + [terms] * 4,
    )(exchange(send, axis), scale)
    return exchange(ends, axis)


def on_device(
    cotangent, concentration, conductance, diffusivity, rate_constant, reactants, products
):
    rows_x, rows_y, width = cotangent.shape
    depth = conductance.shape[2]
    species = diffusivity.shape[0]
    reactions = rate_constant.shape[0]
    columns = rows_x * rows_y * depth
    diffusivity = diffusivity[None, :]
    turn = pltpu.VMEM((width, 2 * rows_x * rows_y), jnp.float32)
    block = struct(CELLS, CELLS, width)
    send = struct(CELLS * (width // LANES) * ROWS, LANES)

    send_y, scale = call(
        functools.partial(start_kernel, depth),
        [send, struct(CELLS, LANES)],
        [
            pltpu.VMEM(cotangent.shape, jnp.float32),
            pltpu.VMEM(conductance.shape, jnp.float32),
            pltpu.VMEM(diffusivity.shape, jnp.float32),
            pltpu.SemaphoreType.DMA((3,)),
        ],
        far_in=(0, 1, 2),
    )(cotangent, conductance, diffusivity)
    count = columns // LANES
    tile = (species * species, LANES)
    jacobian, jacobian_near, inverse, local_y, ends_y, ends_x, sweep_x, packed_x = call(
        functools.partial(prepare_kernel, depth),
        [
            pltpu.HBM((count - NEAR, *tile), jnp.float32),
            struct(NEAR, *tile),
            struct(species, columns),
            block,
            struct(2, CELLS, CELLS, width),
            struct(2, CELLS, CELLS, width),
            struct(5, CELLS, CELLS, width),
            struct(CELLS, LANES),
        ],
        [
            pltpu.VMEM(cotangent.shape, jnp.float32),
            pltpu.VMEM(concentration.shape, jnp.float32),
            pltpu.VMEM(conductance.shape, jnp.float32),
            pltpu.VMEM(diffusivity.shape, jnp.float32),
            pltpu.VMEM((1, reactions), jnp.float32),
            pltpu.VMEM((2, reactions), jnp.int32),
            pltpu.VMEM((2, reactions), jnp.int32),
            turn,
            pltpu.VMEM((2 * reactions, columns), jnp.bfloat16),
            pltpu.VMEM((species * species, 2 * reactions), jnp.bfloat16),
            pltpu.VMEM((count - NEAR, *tile), jnp.float32),
            pltpu.SemaphoreType.DMA((7,)),
            pltpu.SemaphoreType.DMA((count - NEAR,)),
        ],
        far_in=tuple(range(7)),
        far_out=(0,),
    )(
        cotangent,
        concentration,
        conductance,
        diffusivity,
        rate_constant[None, :],
        reactants.T,
        products.T,
    )
    got_y = solve_lines(send_y, scale, "gy", depth)
    send_x, sources = call(
        functools.partial(middle_kernel, depth),
        [send, block],
        [
            turn,
            pltpu.VMEM((species, columns), jnp.float32),
            pltpu.VMEM((count - NEAR, *tile), jnp.float32),
            pltpu.SemaphoreType.DMA((count - NEAR,)),
        ],
        far_in=(3,),
    )(got_y, local_y, ends_y, jacobian, jacobian_near, inverse, ends_x, packed_x)
    got_x = solve_lines(send_x, scale, "gx", depth)
    return call(finish_kernel, block)(got_x, sources, sweep_x)


def solution(mesh):
    placed = (P("gx", "gy", None), P("gx", "gy", None), P("gx", "gy", None), P(), P(), P(), P())
    return jax.shard_map(
        on_device, mesh=mesh, in_specs=placed, out_specs=P("gx", "gy", None), check_vma=False
    )
```

```python
import functools

import jax
import jax.numpy as jnp
from jax import lax
from jax.experimental import pallas as pl
from jax.experimental.pallas import tpu as pltpu
from jax.sharding import PartitionSpec as P


CELLS = 8
LANES = 128
ROWS = 4
NEAR = 5
LIMIT = 16 << 20


def call(kernel, out_shape, scratch_shapes=(), far_in=(), far_out=()):
    near = pl.BlockSpec(memory_space=pltpu.VMEM)
    far = pl.BlockSpec(memory_space=pltpu.HBM)

    def run(*operands):
        operands = [
            pltpu.with_memory_space_constraint(x, pltpu.HBM) if k in far_in else x
            for k, x in enumerate(operands)
        ]
        outs = near
        if isinstance(out_shape, list):
            outs = [far if k in far_out else near for k in range(len(out_shape))]
        return pl.pallas_call(
            kernel,
            out_shape=out_shape,
            in_specs=[far if k in far_in else near for k in range(len(operands))],
            out_specs=outs,
            scratch_shapes=list(scratch_shapes),
            compiler_params=pltpu.CompilerParams(vmem_limit_bytes=LIMIT),
        )(*operands)

    return run


def struct(*shape):
    return jax.ShapeDtypeStruct(shape, jnp.float32)


def begin(pairs, sem):
    copies = [pltpu.make_async_copy(*pair, sem.at[k]) for k, pair in enumerate(pairs)]
    for copy in copies:
        copy.start()
    return copies


def copied(values, source_of, width):
    high = values.astype(jnp.bfloat16)
    rest = values - high.astype(jnp.float32)
    middle = rest.astype(jnp.bfloat16)
    low = (rest - middle.astype(jnp.float32)).astype(jnp.bfloat16)
    count = values.shape[1]
    lane = lax.broadcasted_iota(jnp.int32, (3 * count, width), 1)
    row = lax.broadcasted_iota(jnp.int32, (3 * count, width), 0)
    same = (source_of(lane) == lax.rem(row, count)).astype(jnp.bfloat16)
    parts = jnp.concatenate([high, middle, low], axis=1)
    return jnp.dot(parts, same, preferred_element_type=jnp.float32)


def species_scale(diffusivity, width, depth):
    inverse = jnp.broadcast_to(1.0 / diffusivity, (2 * CELLS, width // depth))
    return copied(inverse, lambda lane: lax.div(lane, depth), width)[:CELLS]


def cell_rates(cond, scale, depth):
    width = scale.shape[1]
    inverse = (1.0 / cond).reshape(-1, depth)
    tiles = copied(inverse, lambda lane: lax.rem(lane, depth), width).reshape(CELLS, CELLS, width)
    return [tiles[cell] * scale for cell in range(CELLS)]


def shoot(rates, value, step, order):
    values = [None] * CELLS
    for cell in order:
        values[cell] = value
        step = step + rates[cell] * value
        value = value + step
    return values, value, step


def factors(rates):
    one = jnp.ones_like(rates[0])
    left, out, _ = shoot(rates, one, one, range(CELLS))
    right, _, _ = shoot(rates, one, one, reversed(range(CELLS)))
    inverse = 1.0 / out
    return [value * inverse for value in right], [value * inverse for value in left]


def sweep_factors(to_first, to_last):
    ratio = to_last[0] * 0.0
    forward = [to_last[k] / to_last[k + 1] for k in range(CELLS - 1)] + [ratio]
    backward = [ratio] + [to_first[k] / to_first[k - 1] for k in range(1, CELLS)]
    scale = 1.0 / to_first[CELLS - 1]
    gains = [to_first[k] * to_last[k] * scale for k in range(CELLS)]
    return forward, backward, gains


def local_solution(sources, forward, backward, gains):
    before, after = [None] * CELLS, [None] * CELLS
    running = sources[0] * 0.0
    for k in range(CELLS):
        before[k] = sources[k] + running
        running = forward[k] * before[k]
    running = sources[0] * 0.0
    for k in reversed(range(CELLS)):
        after[k] = running
        running = backward[k] * (sources[k] + running)
    return [(before[k] + after[k]) * gains[k] for k in range(CELLS)]


def total(weights, sources):
    terms = [weight * source for weight, source in zip(weights, sources, strict=True)]
    while len(terms) > 1:
        terms = [a + b for a, b in zip(terms[::2], terms[1::2], strict=True)]
    return terms[0]


def put_rows(send_ref, rows):
    for row, value in enumerate(rows):
        for tile in range(4):
            part = value
            if value.shape[1] > LANES:
                part = value[:, tile * LANES : (tile + 1) * LANES]
            send_ref[pl.ds(tile * ROWS + row, CELLS, stride=4 * ROWS), :] = part


def pack(cond):
    return jnp.concatenate([cond[cell] for cell in range(CELLS)], axis=1)


def get_ends(back_ref):
    return [
        jnp.concatenate(
            [back_ref[pl.ds(tile * 2 + side, CELLS, stride=CELLS), :] for tile in range(4)], axis=1
        )
        for side in range(2)
    ]


def start_kernel(
    depth, cot_from, cond_from, diffusivity_from, send_ref, scale_ref, cot_ref, cond_ref,
    diffusivity_ref, sem,
):
    width = cot_ref.shape[2]
    copies = begin(
        [(cond_from, cond_ref), (diffusivity_from, diffusivity_ref), (cot_from, cot_ref)], sem
    )
    copies[0].wait()
    copies[1].wait()
    cond = jnp.swapaxes(cond_ref[...], 0, 1)
    scale = species_scale(diffusivity_ref[...], width, depth)
    to_first, to_last = factors(cell_rates(cond, scale, depth))
    packed = pack(cond)
    for tile in range(4):
        scale_ref[pl.ds(tile, 1), :] = scale[0:1, tile * LANES : (tile + 1) * LANES]
    copies[2].wait()
    lines = jnp.swapaxes(cot_ref[...], 0, 1)
    sources = [lines[cell] for cell in range(CELLS)]
    put_rows(
        send_ref,
        [total(to_first, sources), total(to_last, sources), packed, jnp.zeros_like(packed)],
    )


def solve_kernel(depth, axis, blocks, tiles, got_ref, scale_ref, out_ref, *scratch):
    value_l, step_l, value_r, step_r, ratio_l, add_l, ratio_r, add_r, sum_l, sum_r = scratch[:10]
    moves = scratch[10:]
    me = lax.axis_index(axis)
    one = jnp.ones((1, LANES), jnp.float32)

    def whole(tile, row):
        return got_ref[pl.ds(tile * ROWS + row, blocks, stride=ROWS * tiles), :]

    for tile in range(tiles):
        scale = scale_ref[pl.ds(lax.rem(me * tiles + tile, 4), 1), :]
        inverse = 1.0 / whole(tile, 2)
        lane = lax.rem(lax.broadcasted_iota(jnp.int32, inverse.shape, 1), depth)
        rates = [
            jnp.take_along_axis(
                inverse, lane + cell * depth, axis=1, mode="promise_in_bounds"
            )
            * scale
            for cell in range(CELLS)
        ]
        ones = jnp.ones_like(inverse)
        flat, _, flat_step = shoot(rates, ones, ones * 0.0, range(CELLS))
        slope, _, slope_step = shoot(rates, ones * 0.0, ones, range(CELLS))
        last = CELLS - 1
        for move, value in zip(moves, (flat_step, slope_step, flat[last], slope[last]), strict=True):
            move[tile] = value
    for tile in range(tiles):
        left, left_step, right, right_step = one, one, one, one
        for block in range(blocks):
            mirror = blocks - 1 - block
            value_l[tile, pl.ds(block, 1), :] = left
            step_l[tile, pl.ds(block, 1), :] = left_step
            value_r[tile, pl.ds(mirror + 1, 1), :] = right
            step_r[tile, pl.ds(mirror + 1, 1), :] = right_step
            c, d, e, f = (move[tile, pl.ds(block, 1), :] for move in moves)
            kept = e * left + f * left_step
            left_step = c * left + d * left_step
            left = kept + left_step
            c, d, e, f = (move[tile, pl.ds(mirror, 1), :] for move in moves)
            kept = d * right + f * right_step
            right_step = c * right + e * right_step
            right = kept + right_step
        value_l[tile, pl.ds(blocks, 1), :] = left
        step_l[tile, pl.ds(blocks, 1), :] = left_step
        value_r[tile, pl.ds(0, 1), :] = right
        step_r[tile, pl.ds(0, 1), :] = right_step
    for tile in range(tiles):
        near = pl.ds(0, blocks)
        far = pl.ds(1, blocks)
        first, last = whole(tile, 0), whole(tile, 1)
        inverse = 1.0 / value_l[tile, far, :]
        at = value_l[tile, near, :]
        ratio_l[tile] = at * inverse
        add_l[tile] = last + (at - step_l[tile, near, :]) * inverse * first
        inverse = 1.0 / value_r[tile, near, :]
        at = value_r[tile, far, :]
        ratio_r[tile] = at * inverse
        add_r[tile] = first + (at - step_r[tile, far, :]) * inverse * last
    for tile in range(tiles):
        left = jnp.zeros_like(one)
        right = jnp.zeros_like(one)
        for block in range(blocks):
            mirror = blocks - 1 - block
            sum_l[tile, pl.ds(block, 1), :] = left
            sum_r[tile, pl.ds(mirror + 1, 1), :] = right
            here, there = pl.ds(block, 1), pl.ds(mirror, 1)
            left = ratio_l[tile, here, :] * left + add_l[tile, here, :]
            right = ratio_r[tile, there, :] * right + add_r[tile, there, :]
        sum_l[tile, pl.ds(blocks, 1), :] = left
        sum_r[tile, pl.ds(0, 1), :] = right
    for tile in range(tiles):
        for side in range(2):
            rows = pl.ds(side, blocks)
            gap_l = step_l[tile, rows, :] / value_l[tile, rows, :]
            gap_r = step_r[tile, rows, :] / value_r[tile, rows, :]
            inverse = 1.0 / (gap_l + gap_r * (1.0 - gap_l))
            left, right = sum_l[tile, rows, :], sum_r[tile, rows, :]
            if side == 0:
                ends = (left + (1.0 - gap_l) * right) * inverse
            else:
                ends = (right + (1.0 - gap_r) * left) * inverse
            out_ref[pl.ds(tile * 2 + side, blocks, stride=2 * tiles), :] = ends


def to_species(cells, turn_ref, depth):
    rows = cells.shape[0]
    turn_ref[...] = jnp.concatenate([cells, cells], axis=0).T
    species = cells.shape[1] // depth
    low = lax.broadcasted_iota(jnp.int32, (species, 2 * rows), 1) < rows
    pairs = []
    for pair in range(depth // 2):
        even = turn_ref[pl.ds(2 * pair, species, stride=depth), :]
        odd = turn_ref[pl.ds(2 * pair + 1, species, stride=depth), :]
        pairs.append(jnp.where(low, even, odd))
    return pairs


def from_species(pairs, turn_ref, depth):
    species, columns = pairs[0].shape
    for pair, tile in enumerate(pairs):
        turn_ref[pl.ds(2 * pair, species, stride=depth), :] = tile
        turn_ref[pl.ds(2 * pair + 1, species, stride=depth), :] = pltpu.roll(
            tile, columns // 2, 1
        )
    return turn_ref[...].T[: columns // 2]


def halves(value):
    high = value.astype(jnp.bfloat16)
    return high, (value - high.astype(jnp.float32)).astype(jnp.bfloat16)


def counts(pair_ref, species):
    ids = lax.broadcasted_iota(jnp.int32, (pair_ref.shape[0], species), 1)
    return (pair_ref[:, 0:1] == ids).astype(jnp.float32) + (pair_ref[:, 1:2] == ids).astype(
        jnp.float32
    )


def counts(pair_ref, species):
    ids = lax.broadcasted_iota(jnp.int32, (species, pair_ref.shape[1]), 0)
    return (pair_ref[0:1, :] == ids).astype(jnp.float32) + (pair_ref[1:2, :] == ids).astype(
        jnp.float32
    )


def prepare_kernel(
    depth, cot_from, conc_from, cond_from, diffusivity_from, rate_from, reactants_from,
    products_from, jacobian_to, sweep_x_to, jacobian_near_ref, local_y_ref, ends_y_ref,
    ends_x_ref, packed_x_ref, cot_ref, conc_ref, cond_ref, diffusivity_ref, rate_ref,
    reactants_ref, products_ref, turn_ref, rates_ref, pairs_ref, inverse_ref, sweep_x_ref,
    jacobian_ref, in_sem, sem,
):
    inputs = begin(
        [
            (reactants_from, reactants_ref),
            (products_from, products_ref),
            (rate_from, rate_ref),
            (conc_from, conc_ref),
            (cond_from, cond_ref),
            (diffusivity_from, diffusivity_ref),
            (cot_from, cot_ref),
        ],
        in_sem,
    )
    for copy in inputs:
        copy.wait()
    rows_x, rows_y, width = conc_ref.shape
    species = width // depth
    used = counts(reactants_ref, species)
    net = counts(products_ref, species) - used
    for s in range(species):
        product = (net[s : s + 1, :] * used).astype(jnp.bfloat16)
        rows = pl.ds(s * species, species)
        pairs_ref[rows, : used.shape[1]] = product
        pairs_ref[rows, used.shape[1] :] = product
    twice = jnp.concatenate([used, used], axis=0).T.astype(jnp.bfloat16)
    constant = jnp.broadcast_to(rate_ref[...], (LANES, rate_ref.shape[1])).T
    pairs = to_species(conc_ref[...].reshape(rows_x * rows_y, width), turn_ref, depth)
    for pair, conc in enumerate(pairs):
        columns = pl.ds(pair * conc.shape[1], conc.shape[1])
        inverse_ref[:, columns] = 1.0 / conc
        stacked = jnp.concatenate(halves(jnp.log(conc)), axis=0)
        exponent = jnp.dot(twice, stacked, preferred_element_type=jnp.float32)
        rates_ref[:, columns] = jnp.concatenate(halves(constant * jnp.exp(exponent)), axis=0)
    wide = 2 * LANES
    copies = []
    for chunk in range(rates_ref.shape[1] // wide):
        columns = pl.ds(chunk * wide, wide)
        block = jnp.dot(pairs_ref[...], rates_ref[:, columns], preferred_element_type=jnp.float32)
        for part in range(2):
            tile = 2 * chunk + part - jacobian_ref.shape[0]
            here = pl.ds((2 * chunk + part) * LANES, LANES)
            value = block[:, part * LANES : (part + 1) * LANES].reshape(species, species, LANES)
            value = (value * inverse_ref[:, here][None]).reshape(-1, LANES)
            if tile >= 0:
                jacobian_near_ref[tile] = value
                continue
            tile += jacobian_ref.shape[0]
            jacobian_ref[tile] = value
            copies.append(
                pltpu.make_async_copy(jacobian_ref.at[tile], jacobian_to.at[tile], sem.at[tile])
            )
            copies[-1].start()

    cond = cond_ref[...]
    scale = species_scale(diffusivity_ref[...], width, depth)
    packed_x_ref[...] = pack(cond)
    rates = cell_rates(cond, scale, depth)
    to_first, to_last = factors(rates)
    forward, backward, gains = sweep_factors(to_first, to_last)
    for k in range(CELLS):
        ends_x_ref[0, k] = to_first[k]
        ends_x_ref[1, k] = to_last[k]
        sweep_x_ref[0, k] = forward[k]
        sweep_x_ref[1, k] = backward[k]
        sweep_x_ref[2, k] = gains[k] * rates[k]
        sweep_x_ref[3, k] = to_first[k] * rates[k]
        sweep_x_ref[4, k] = to_last[k] * rates[k]
    copies.append(
        pltpu.make_async_copy(sweep_x_ref, sweep_x_to, sem.at[jacobian_ref.shape[0]])
    )
    copies[-1].start()
    rates = cell_rates(jnp.swapaxes(cond, 0, 1), scale, depth)
    to_first, to_last = factors(rates)
    lines = jnp.swapaxes(cot_ref[...], 0, 1)
    local = local_solution([lines[k] for k in range(CELLS)], *sweep_factors(to_first, to_last))
    for k in range(CELLS):
        local_y_ref[k] = local[k] * rates[k]
        ends_y_ref[0, k] = to_first[k] * rates[k]
        ends_y_ref[1, k] = to_last[k] * rates[k]
    for copy in copies:
        copy.wait()


def chemistry(field, columns, jacobian_ref, vector_ref):
    species = field.shape[0]

    def transposed(vector):
        vector_ref[:, columns] = vector
        sums = [None] * 4
        for s in range(species):
            row = jnp.broadcast_to(vector_ref[pl.ds(s, 1), columns], vector.shape)
            term = row * jacobian_ref[pl.ds(s * species, species), :]
            sums[s % 4] = term if sums[s % 4] is None else sums[s % 4] + term
        return (sums[0] + sums[1]) + (sums[2] + sums[3])

    third = field + transposed(field) * (1.0 / 3.0)
    second = field + transposed(third) * 0.5
    return field + transposed(second)


def middle_kernel(
    depth, ends_ref, local_ref, ends_y_ref, jacobian_from, jacobian_near_ref, ends_x_ref,
    packed_x_ref, sweep_from, send_ref, sources_ref, sweep_ref, turn_ref, vector_ref,
    jacobian_ref, sem,
):
    width = local_ref.shape[2]
    far = jacobian_ref.shape[0]
    copies = begin(
        [
            *((jacobian_from.at[tile], jacobian_ref.at[tile]) for tile in range(far)),
            (sweep_from, sweep_ref),
        ],
        sem,
    )
    left, right = get_ends(ends_ref)
    solved = jnp.stack(
        [
            local_ref[k] + ends_y_ref[0, k] * left + ends_y_ref[1, k] * right
            for k in range(CELLS)
        ],
        axis=0,
    )
    solved = jnp.swapaxes(solved, 0, 1).reshape(CELLS * CELLS, width)
    pairs = to_species(solved, turn_ref, depth)
    done = [None] * len(pairs)
    for pair in [*range(far, len(pairs)), *range(far)]:
        field = pairs[pair]
        columns = pl.ds(pair * field.shape[1], field.shape[1])
        if pair < far:
            copies[pair].wait()
            jacobian = jacobian_ref.at[pair]
        else:
            jacobian = jacobian_near_ref.at[pair - far]
        done[pair] = chemistry(field, columns, jacobian, vector_ref)
    changed = from_species(done, turn_ref, depth).reshape(CELLS, CELLS, width)
    sources_ref[...] = changed
    sources = [changed[k] for k in range(CELLS)]
    packed = packed_x_ref[...]
    put_rows(
        send_ref,
        [
            total([ends_x_ref[0, k] for k in range(CELLS)], sources),
            total([ends_x_ref[1, k] for k in range(CELLS)], sources),
            packed,
            jnp.zeros_like(packed),
        ],
    )
    copies[far].wait()


def finish_kernel(ends_ref, sources_ref, sweep_ref, out_ref):
    local = local_solution(
        [sources_ref[k] for k in range(CELLS)],
        *([sweep_ref[part, k] for k in range(CELLS)] for part in range(3)),
    )
    left, right = get_ends(ends_ref)
    for k in range(CELLS):
        out_ref[k] = local[k] + sweep_ref[3, k] * left + sweep_ref[4, k] * right


def exchange(rows, axis):
    members = lax.axis_size(axis)
    blocks = rows.reshape(members, rows.shape[0] // members, LANES)
    return lax.all_to_all(blocks, axis, 0, 0, tiled=True).reshape(rows.shape)


def solve_lines(send, scale, axis, depth):
    blocks = lax.axis_size(axis)
    tiles = send.shape[0] // (blocks * ROWS)
    states = pltpu.VMEM((tiles, blocks + CELLS, LANES), jnp.float32)
    terms = pltpu.VMEM((tiles, blocks, LANES), jnp.float32)
    ends = call(
        functools.partial(solve_kernel, depth, axis, blocks, tiles),
        struct(2 * blocks * tiles, LANES),
        [states] * 4 + [terms] * 4 + [states] * 2 + [terms] * 4,
    )(exchange(send, axis), scale)
    return exchange(ends, axis)


def on_device(
    cotangent, concentration, conductance, diffusivity, rate_constant, reactants, products
):
    rows_x, rows_y, width = cotangent.shape
    depth = conductance.shape[2]
    species = diffusivity.shape[0]
    reactions = rate_constant.shape[0]
    columns = rows_x * rows_y * depth
    diffusivity = diffusivity[None, :]
    turn = pltpu.VMEM((width, 2 * rows_x * rows_y), jnp.float32)
    block = struct(CELLS, CELLS, width)
    send = struct(CELLS * (width // LANES) * ROWS, LANES)

    send_y, scale = call(
        functools.partial(start_kernel, depth),
        [send, struct(CELLS, LANES)],
        [
            pltpu.VMEM(cotangent.shape, jnp.float32),
            pltpu.VMEM(conductance.shape, jnp.float32),
            pltpu.VMEM(diffusivity.shape, jnp.float32),
            pltpu.SemaphoreType.DMA((3,)),
        ],
        far_in=(0, 1, 2),
    )(cotangent, conductance, diffusivity)
    count = columns // LANES
    tile = (species * species, LANES)
    sweep = (5, CELLS, CELLS, width)
    jacobian, sweep_x, jacobian_near, local_y, ends_y, ends_x, packed_x = call(
        functools.partial(prepare_kernel, depth),
        [
            pltpu.HBM((count - NEAR, *tile), jnp.float32),
            pltpu.HBM(sweep, jnp.float32),
            struct(NEAR, *tile),
            block,
            struct(2, CELLS, CELLS, width),
            struct(2, CELLS, CELLS, width),
            struct(CELLS, LANES),
        ],
        [
            pltpu.VMEM(cotangent.shape, jnp.float32),
            pltpu.VMEM(concentration.shape, jnp.float32),
            pltpu.VMEM(conductance.shape, jnp.float32),
            pltpu.VMEM(diffusivity.shape, jnp.float32),
            pltpu.VMEM((1, reactions), jnp.float32),
            pltpu.VMEM((2, reactions), jnp.int32),
            pltpu.VMEM((2, reactions), jnp.int32),
            turn,
            pltpu.VMEM((2 * reactions, columns), jnp.bfloat16),
            pltpu.VMEM((species * species, 2 * reactions), jnp.bfloat16),
            pltpu.VMEM((species, columns), jnp.float32),
            pltpu.VMEM(sweep, jnp.float32),
            pltpu.VMEM((count - NEAR, *tile), jnp.float32),
            pltpu.SemaphoreType.DMA((7,)),
            pltpu.SemaphoreType.DMA((count - NEAR + 1,)),
        ],
        far_in=tuple(range(7)),
        far_out=(0, 1),
    )(
        cotangent,
        concentration,
        conductance,
        diffusivity,
        rate_constant[None, :],
        reactants.T,
        products.T,
    )
    got_y = solve_lines(send_y, scale, "gy", depth)
    send_x, sources, sweep_x = call(
        functools.partial(middle_kernel, depth),
        [send, block, struct(*sweep)],
        [
            turn,
            pltpu.VMEM((species, columns), jnp.float32),
            pltpu.VMEM((count - NEAR, *tile), jnp.float32),
            pltpu.SemaphoreType.DMA((count - NEAR + 1,)),
        ],
        far_in=(3, 7),
    )(got_y, local_y, ends_y, jacobian, jacobian_near, ends_x, packed_x, sweep_x)
    got_x = solve_lines(send_x, scale, "gx", depth)
    return call(finish_kernel, block)(got_x, sources, sweep_x)


def solution(mesh):
    placed = (P("gx", "gy", None), P("gx", "gy", None), P("gx", "gy", None), P(), P(), P(), P())
    return jax.shard_map(
        on_device, mesh=mesh, in_specs=placed, out_specs=P("gx", "gy", None), check_vma=False
    )
```

```python
import functools

import jax
import jax.numpy as jnp
from jax import lax
from jax.experimental import pallas as pl
from jax.experimental.pallas import tpu as pltpu
from jax.sharding import PartitionSpec as P


CELLS = 8
LANES = 128
ROWS = 4
NEAR = 5
LIMIT = 16 << 20


def call(kernel, out_shape, scratch_shapes=(), far_in=(), far_out=()):
    near = pl.BlockSpec(memory_space=pltpu.VMEM)
    far = pl.BlockSpec(memory_space=pltpu.HBM)

    def run(*operands):
        operands = [
            pltpu.with_memory_space_constraint(x, pltpu.HBM) if k in far_in else x
            for k, x in enumerate(operands)
        ]
        outs = near
        if isinstance(out_shape, list):
            outs = [far if k in far_out else near for k in range(len(out_shape))]
        return pl.pallas_call(
            kernel,
            out_shape=out_shape,
            in_specs=[far if k in far_in else near for k in range(len(operands))],
            out_specs=outs,
            scratch_shapes=list(scratch_shapes),
            compiler_params=pltpu.CompilerParams(vmem_limit_bytes=LIMIT),
        )(*operands)

    return run


def struct(*shape):
    return jax.ShapeDtypeStruct(shape, jnp.float32)


def begin(pairs, sem):
    copies = [pltpu.make_async_copy(*pair, sem.at[k]) for k, pair in enumerate(pairs)]
    for copy in copies:
        copy.start()
    return copies


def copied(values, source_of, width):
    high = values.astype(jnp.bfloat16)
    rest = values - high.astype(jnp.float32)
    middle = rest.astype(jnp.bfloat16)
    low = (rest - middle.astype(jnp.float32)).astype(jnp.bfloat16)
    count = values.shape[1]
    lane = lax.broadcasted_iota(jnp.int32, (3 * count, width), 1)
    row = lax.broadcasted_iota(jnp.int32, (3 * count, width), 0)
    same = (source_of(lane) == lax.rem(row, count)).astype(jnp.bfloat16)
    parts = jnp.concatenate([high, middle, low], axis=1)
    return jnp.dot(parts, same, preferred_element_type=jnp.float32)


def species_scale(diffusivity, width, depth):
    inverse = jnp.broadcast_to(1.0 / diffusivity, (2 * CELLS, width // depth))
    return copied(inverse, lambda lane: lax.div(lane, depth), width)[:CELLS]


def cell_rates(cond, scale, depth):
    width = scale.shape[1]
    inverse = (1.0 / cond).reshape(-1, depth)
    tiles = copied(inverse, lambda lane: lax.rem(lane, depth), width).reshape(CELLS, CELLS, width)
    return [tiles[cell] * scale for cell in range(CELLS)]


def shoot(rates, value, step, order):
    values = [None] * CELLS
    for cell in order:
        values[cell] = value
        step = step + rates[cell] * value
        value = value + step
    return values, value, step


def factors(rates):
    one = jnp.ones_like(rates[0])
    left, out, _ = shoot(rates, one, one, range(CELLS))
    right, _, _ = shoot(rates, one, one, reversed(range(CELLS)))
    inverse = 1.0 / out
    return [value * inverse for value in right], [value * inverse for value in left]


def local_solution(sources, to_first, to_last):
    scale = 1.0 / to_first[CELLS - 1]
    before, after = [None] * CELLS, [None] * CELLS
    running = to_last[0] * sources[0]
    for k in range(CELLS):
        running = running if k == 0 else running + to_last[k] * sources[k]
        before[k] = running
    running = jnp.zeros_like(scale)
    for k in reversed(range(CELLS)):
        after[k] = running
        running = running + to_first[k] * sources[k]
    return [(to_first[k] * before[k] + to_last[k] * after[k]) * scale for k in range(CELLS)]


def total(weights, sources):
    terms = [weight * source for weight, source in zip(weights, sources, strict=True)]
    while len(terms) > 1:
        terms = [a + b for a, b in zip(terms[::2], terms[1::2], strict=True)]
    return terms[0]


def put_rows(send_ref, rows):
    for row, value in enumerate(rows):
        for tile in range(4):
            part = value
            if value.shape[1] > LANES:
                part = value[:, tile * LANES : (tile + 1) * LANES]
            send_ref[pl.ds(tile * ROWS + row, CELLS, stride=4 * ROWS), :] = part


def pack(cond):
    return jnp.concatenate([cond[cell] for cell in range(CELLS)], axis=1)


def get_ends(back_ref):
    return [
        jnp.concatenate(
            [back_ref[pl.ds(tile * 2 + side, CELLS, stride=CELLS), :] for tile in range(4)], axis=1
        )
        for side in range(2)
    ]


def start_kernel(
    depth, cot_from, cond_from, diffusivity_from, send_ref, scale_ref, cot_ref, cond_ref,
    diffusivity_ref, sem,
):
    width = cot_ref.shape[2]
    copies = begin(
        [
            (cond_from, cond_ref),
            (diffusivity_from, diffusivity_ref),
            *((cot_from.at[pl.ds(k, 2)], cot_ref.at[pl.ds(k, 2)]) for k in range(0, CELLS, 2)),
        ],
        sem,
    )
    copies[0].wait()
    copies[1].wait()
    cond = jnp.swapaxes(cond_ref[...], 0, 1)
    scale = species_scale(diffusivity_ref[...], width, depth)
    to_first, to_last = factors(cell_rates(cond, scale, depth))
    packed = pack(cond)
    for tile in range(4):
        scale_ref[pl.ds(tile, 1), :] = scale[0:1, tile * LANES : (tile + 1) * LANES]
    for copy in copies[2:]:
        copy.wait()
    lines = jnp.swapaxes(cot_ref[...], 0, 1)
    sources = [lines[cell] for cell in range(CELLS)]
    put_rows(
        send_ref,
        [total(to_first, sources), total(to_last, sources), packed, jnp.zeros_like(packed)],
    )


def solve_kernel(depth, axis, blocks, tiles, got_ref, scale_ref, out_ref, *scratch):
    value_l, step_l, value_r, step_r, ratio_l, add_l, ratio_r, add_r, sum_l, sum_r = scratch[:10]
    moves = scratch[10:]
    me = lax.axis_index(axis)
    one = jnp.ones((1, LANES), jnp.float32)

    def whole(tile, row):
        return got_ref[pl.ds(tile * ROWS + row, blocks, stride=ROWS * tiles), :]

    for tile in range(tiles):
        scale = scale_ref[pl.ds(lax.rem(me * tiles + tile, 4), 1), :]
        inverse = 1.0 / whole(tile, 2)
        lane = lax.rem(lax.broadcasted_iota(jnp.int32, inverse.shape, 1), depth)
        rates = [
            jnp.take_along_axis(
                inverse, lane + cell * depth, axis=1, mode="promise_in_bounds"
            )
            * scale
            for cell in range(CELLS)
        ]
        ones = jnp.ones_like(inverse)
        flat, _, flat_step = shoot(rates, ones, ones * 0.0, range(CELLS))
        slope, _, slope_step = shoot(rates, ones * 0.0, ones, range(CELLS))
        last = CELLS - 1
        for move, value in zip(moves, (flat_step, slope_step, flat[last], slope[last]), strict=True):
            move[tile] = value
    for tile in range(tiles):
        left, left_step, right, right_step = one, one, one, one
        for block in range(blocks):
            mirror = blocks - 1 - block
            value_l[tile, pl.ds(block, 1), :] = left
            step_l[tile, pl.ds(block, 1), :] = left_step
            value_r[tile, pl.ds(mirror + 1, 1), :] = right
            step_r[tile, pl.ds(mirror + 1, 1), :] = right_step
            c, d, e, f = (move[tile, pl.ds(block, 1), :] for move in moves)
            kept = e * left + f * left_step
            left_step = c * left + d * left_step
            left = kept + left_step
            c, d, e, f = (move[tile, pl.ds(mirror, 1), :] for move in moves)
            kept = d * right + f * right_step
            right_step = c * right + e * right_step
            right = kept + right_step
        value_l[tile, pl.ds(blocks, 1), :] = left
        step_l[tile, pl.ds(blocks, 1), :] = left_step
        value_r[tile, pl.ds(0, 1), :] = right
        step_r[tile, pl.ds(0, 1), :] = right_step
    for tile in range(tiles):
        near = pl.ds(0, blocks)
        far = pl.ds(1, blocks)
        first, last = whole(tile, 0), whole(tile, 1)
        inverse = 1.0 / value_l[tile, far, :]
        at = value_l[tile, near, :]
        ratio_l[tile] = at * inverse
        add_l[tile] = last + (at - step_l[tile, near, :]) * inverse * first
        inverse = 1.0 / value_r[tile, near, :]
        at = value_r[tile, far, :]
        ratio_r[tile] = at * inverse
        add_r[tile] = first + (at - step_r[tile, far, :]) * inverse * last
    for tile in range(tiles):
        left = jnp.zeros_like(one)
        right = jnp.zeros_like(one)
        for block in range(blocks):
            mirror = blocks - 1 - block
            sum_l[tile, pl.ds(block, 1), :] = left
            sum_r[tile, pl.ds(mirror + 1, 1), :] = right
            here, there = pl.ds(block, 1), pl.ds(mirror, 1)
            left = ratio_l[tile, here, :] * left + add_l[tile, here, :]
            right = ratio_r[tile, there, :] * right + add_r[tile, there, :]
        sum_l[tile, pl.ds(blocks, 1), :] = left
        sum_r[tile, pl.ds(0, 1), :] = right
    for tile in range(tiles):
        for side in range(2):
            rows = pl.ds(side, blocks)
            gap_l = step_l[tile, rows, :] / value_l[tile, rows, :]
            gap_r = step_r[tile, rows, :] / value_r[tile, rows, :]
            inverse = 1.0 / (gap_l + gap_r * (1.0 - gap_l))
            left, right = sum_l[tile, rows, :], sum_r[tile, rows, :]
            if side == 0:
                ends = (left + (1.0 - gap_l) * right) * inverse
            else:
                ends = (right + (1.0 - gap_r) * left) * inverse
            out_ref[pl.ds(tile * 2 + side, blocks, stride=2 * tiles), :] = ends


def to_species(cells, turn_ref, depth):
    rows = cells.shape[0]
    turn_ref[...] = jnp.concatenate([cells, cells], axis=0).T
    species = cells.shape[1] // depth
    low = lax.broadcasted_iota(jnp.int32, (species, 2 * rows), 1) < rows
    pairs = []
    for pair in range(depth // 2):
        even = turn_ref[pl.ds(2 * pair, species, stride=depth), :]
        odd = turn_ref[pl.ds(2 * pair + 1, species, stride=depth), :]
        pairs.append(jnp.where(low, even, odd))
    return pairs


def from_species(pairs, turn_ref, depth):
    species, columns = pairs[0].shape
    for pair, tile in enumerate(pairs):
        turn_ref[pl.ds(2 * pair, species, stride=depth), :] = tile
        turn_ref[pl.ds(2 * pair + 1, species, stride=depth), :] = pltpu.roll(
            tile, columns // 2, 1
        )
    return turn_ref[...].T[: columns // 2]


def halves(value):
    high = value.astype(jnp.bfloat16)
    return high, (value - high.astype(jnp.float32)).astype(jnp.bfloat16)


def counts(pair_ref, species):
    ids = lax.broadcasted_iota(jnp.int32, (pair_ref.shape[0], species), 1)
    return (pair_ref[:, 0:1] == ids).astype(jnp.float32) + (pair_ref[:, 1:2] == ids).astype(
        jnp.float32
    )


def counts(pair_ref, species):
    ids = lax.broadcasted_iota(jnp.int32, (species, pair_ref.shape[1]), 0)
    return (pair_ref[0:1, :] == ids).astype(jnp.float32) + (pair_ref[1:2, :] == ids).astype(
        jnp.float32
    )


def prepare_kernel(
    depth, cot_from, conc_from, cond_from, diffusivity_from, rate_from, reactants_from,
    products_from, jacobian_to, jacobian_near_ref, local_y_ref, ends_y_ref, ends_x_ref,
    rates_x_ref, packed_x_ref, cot_ref, conc_ref, cond_ref, diffusivity_ref, rate_ref,
    reactants_ref, products_ref, turn_ref, rates_ref, pairs_ref, inverse_ref, jacobian_ref,
    in_sem, sem,
):
    inputs = begin(
        [
            (reactants_from, reactants_ref),
            (products_from, products_ref),
            (rate_from, rate_ref),
            (conc_from, conc_ref),
            (cond_from, cond_ref),
            (diffusivity_from, diffusivity_ref),
            (cot_from, cot_ref),
        ],
        in_sem,
    )
    for copy in inputs:
        copy.wait()
    rows_x, rows_y, width = conc_ref.shape
    species = width // depth
    used = counts(reactants_ref, species)
    net = counts(products_ref, species) - used
    for s in range(species):
        product = (net[s : s + 1, :] * used).astype(jnp.bfloat16)
        rows = pl.ds(s * species, species)
        pairs_ref[rows, : used.shape[1]] = product
        pairs_ref[rows, used.shape[1] :] = product
    twice = jnp.concatenate([used, used], axis=0).T.astype(jnp.bfloat16)
    constant = jnp.broadcast_to(rate_ref[...], (LANES, rate_ref.shape[1])).T
    pairs = to_species(conc_ref[...].reshape(rows_x * rows_y, width), turn_ref, depth)
    for pair, conc in enumerate(pairs):
        columns = pl.ds(pair * conc.shape[1], conc.shape[1])
        inverse_ref[:, columns] = 1.0 / conc
        stacked = jnp.concatenate(halves(jnp.log(conc)), axis=0)
        exponent = jnp.dot(twice, stacked, preferred_element_type=jnp.float32)
        rates_ref[:, columns] = jnp.concatenate(halves(constant * jnp.exp(exponent)), axis=0)
    wide = 2 * LANES
    copies = []
    for chunk in range(rates_ref.shape[1] // wide):
        columns = pl.ds(chunk * wide, wide)
        block = jnp.dot(pairs_ref[...], rates_ref[:, columns], preferred_element_type=jnp.float32)
        for part in range(2):
            tile = 2 * chunk + part - jacobian_ref.shape[0]
            here = pl.ds((2 * chunk + part) * LANES, LANES)
            value = block[:, part * LANES : (part + 1) * LANES].reshape(species, species, LANES)
            value = (value * inverse_ref[:, here][None]).reshape(-1, LANES)
            if tile >= 0:
                jacobian_near_ref[tile] = value
                continue
            tile += jacobian_ref.shape[0]
            jacobian_ref[tile] = value
            copies.append(
                pltpu.make_async_copy(jacobian_ref.at[tile], jacobian_to.at[tile], sem.at[tile])
            )
            copies[-1].start()

    cond = cond_ref[...]
    scale = species_scale(diffusivity_ref[...], width, depth)
    packed_x_ref[...] = pack(cond)
    rates = cell_rates(cond, scale, depth)
    to_first, to_last = factors(rates)
    for k in range(CELLS):
        ends_x_ref[0, k] = to_first[k]
        ends_x_ref[1, k] = to_last[k]
        rates_x_ref[k] = rates[k]
    rates = cell_rates(jnp.swapaxes(cond, 0, 1), scale, depth)
    to_first, to_last = factors(rates)
    lines = jnp.swapaxes(cot_ref[...], 0, 1)
    local = local_solution([lines[k] for k in range(CELLS)], to_first, to_last)
    for k in range(CELLS):
        local_y_ref[k] = local[k] * rates[k]
        ends_y_ref[0, k] = to_first[k] * rates[k]
        ends_y_ref[1, k] = to_last[k] * rates[k]
    for copy in copies:
        copy.wait()


def chemistry(field, columns, jacobian_ref, vector_ref):
    species = field.shape[0]

    def transposed(vector):
        vector_ref[:, columns] = vector
        sums = [None] * 4
        for s in range(species):
            row = jnp.broadcast_to(vector_ref[pl.ds(s, 1), columns], vector.shape)
            term = row * jacobian_ref[pl.ds(s * species, species), :]
            sums[s % 4] = term if sums[s % 4] is None else sums[s % 4] + term
        return (sums[0] + sums[1]) + (sums[2] + sums[3])

    third = field + transposed(field) * (1.0 / 3.0)
    second = field + transposed(third) * 0.5
    return field + transposed(second)


def middle_kernel(
    depth, ends_ref, local_ref, ends_y_ref, jacobian_from, jacobian_near_ref, ends_x_ref,
    packed_x_ref, send_ref, sources_ref, turn_ref, vector_ref, jacobian_ref, sem,
):
    width = local_ref.shape[2]
    far = jacobian_ref.shape[0]
    copies = begin(
        [(jacobian_from.at[tile], jacobian_ref.at[tile]) for tile in range(far)], sem
    )
    left, right = get_ends(ends_ref)
    solved = jnp.stack(
        [
            local_ref[k] + ends_y_ref[0, k] * left + ends_y_ref[1, k] * right
            for k in range(CELLS)
        ],
        axis=0,
    )
    solved = jnp.swapaxes(solved, 0, 1).reshape(CELLS * CELLS, width)
    pairs = to_species(solved, turn_ref, depth)
    done = [None] * len(pairs)
    for pair in [*range(far, len(pairs)), *range(far)]:
        field = pairs[pair]
        columns = pl.ds(pair * field.shape[1], field.shape[1])
        if pair < far:
            copies[pair].wait()
            jacobian = jacobian_ref.at[pair]
        else:
            jacobian = jacobian_near_ref.at[pair - far]
        done[pair] = chemistry(field, columns, jacobian, vector_ref)
    changed = from_species(done, turn_ref, depth).reshape(CELLS, CELLS, width)
    sources_ref[...] = changed
    sources = [changed[k] for k in range(CELLS)]
    packed = packed_x_ref[...]
    put_rows(
        send_ref,
        [
            total([ends_x_ref[0, k] for k in range(CELLS)], sources),
            total([ends_x_ref[1, k] for k in range(CELLS)], sources),
            packed,
            jnp.zeros_like(packed),
        ],
    )


def finish_kernel(ends_ref, sources_ref, ends_x_ref, rates_ref, out_to, out_ref, sem):
    to_first = [ends_x_ref[0, k] for k in range(CELLS)]
    to_last = [ends_x_ref[1, k] for k in range(CELLS)]
    local = local_solution([sources_ref[k] for k in range(CELLS)], to_first, to_last)
    left, right = get_ends(ends_ref)
    copies = []
    for k in range(CELLS):
        out_ref[k] = (local[k] + to_first[k] * left + to_last[k] * right) * rates_ref[k]
        if k % 2:
            pair = pl.ds(k - 1, 2)
            copies.append(pltpu.make_async_copy(out_ref.at[pair], out_to.at[pair], sem.at[k // 2]))
            copies[-1].start()
    for copy in copies:
        copy.wait()


def exchange(rows, axis):
    members = lax.axis_size(axis)
    blocks = rows.reshape(members, rows.shape[0] // members, LANES)
    return lax.all_to_all(blocks, axis, 0, 0, tiled=True).reshape(rows.shape)


def solve_lines(send, scale, axis, depth):
    blocks = lax.axis_size(axis)
    tiles = send.shape[0] // (blocks * ROWS)
    states = pltpu.VMEM((tiles, blocks + CELLS, LANES), jnp.float32)
    terms = pltpu.VMEM((tiles, blocks, LANES), jnp.float32)
    ends = call(
        functools.partial(solve_kernel, depth, axis, blocks, tiles),
        struct(2 * blocks * tiles, LANES),
        [states] * 4 + [terms] * 4 + [states] * 2 + [terms] * 4,
    )(exchange(send, axis), scale)
    return exchange(ends, axis)


def on_device(
    cotangent, concentration, conductance, diffusivity, rate_constant, reactants, products
):
    rows_x, rows_y, width = cotangent.shape
    depth = conductance.shape[2]
    species = diffusivity.shape[0]
    reactions = rate_constant.shape[0]
    columns = rows_x * rows_y * depth
    diffusivity = diffusivity[None, :]
    turn = pltpu.VMEM((width, 2 * rows_x * rows_y), jnp.float32)
    block = struct(CELLS, CELLS, width)
    send = struct(CELLS * (width // LANES) * ROWS, LANES)

    send_y, scale = call(
        functools.partial(start_kernel, depth),
        [send, struct(CELLS, LANES)],
        [
            pltpu.VMEM(cotangent.shape, jnp.float32),
            pltpu.VMEM(conductance.shape, jnp.float32),
            pltpu.VMEM(diffusivity.shape, jnp.float32),
            pltpu.SemaphoreType.DMA((6,)),
        ],
        far_in=(0, 1, 2),
    )(cotangent, conductance, diffusivity)
    count = columns // LANES
    tile = (species * species, LANES)
    jacobian, jacobian_near, local_y, ends_y, ends_x, rates_x, packed_x = call(
        functools.partial(prepare_kernel, depth),
        [
            pltpu.HBM((count - NEAR, *tile), jnp.float32),
            struct(NEAR, *tile),
            block,
            struct(2, CELLS, CELLS, width),
            struct(2, CELLS, CELLS, width),
            block,
            struct(CELLS, LANES),
        ],
        [
            pltpu.VMEM(cotangent.shape, jnp.float32),
            pltpu.VMEM(concentration.shape, jnp.float32),
            pltpu.VMEM(conductance.shape, jnp.float32),
            pltpu.VMEM(diffusivity.shape, jnp.float32),
            pltpu.VMEM((1, reactions), jnp.float32),
            pltpu.VMEM((2, reactions), jnp.int32),
            pltpu.VMEM((2, reactions), jnp.int32),
            turn,
            pltpu.VMEM((2 * reactions, columns), jnp.bfloat16),
            pltpu.VMEM((species * species, 2 * reactions), jnp.bfloat16),
            pltpu.VMEM((species, columns), jnp.float32),
            pltpu.VMEM((count - NEAR, *tile), jnp.float32),
            pltpu.SemaphoreType.DMA((7,)),
            pltpu.SemaphoreType.DMA((count - NEAR,)),
        ],
        far_in=tuple(range(7)),
        far_out=(0,),
    )(
        cotangent,
        concentration,
        conductance,
        diffusivity,
        rate_constant[None, :],
        reactants.T,
        products.T,
    )
    got_y = solve_lines(send_y, scale, "gy", depth)
    send_x, sources = call(
        functools.partial(middle_kernel, depth),
        [send, block],
        [
            turn,
            pltpu.VMEM((species, columns), jnp.float32),
            pltpu.VMEM((count - NEAR, *tile), jnp.float32),
            pltpu.SemaphoreType.DMA((count - NEAR,)),
        ],
        far_in=(3,),
    )(got_y, local_y, ends_y, jacobian, jacobian_near, ends_x, packed_x)
    got_x = solve_lines(send_x, scale, "gx", depth)
    return call(
        finish_kernel,
        [block],
        [pltpu.VMEM(block.shape, jnp.float32), pltpu.SemaphoreType.DMA((CELLS // 2,))],
        far_out=(0,),
    )(got_x, sources, ends_x, rates_x)[0]


def solution(mesh):
    placed = (P("gx", "gy", None), P("gx", "gy", None), P("gx", "gy", None), P(), P(), P(), P())
    return jax.shard_map(
        on_device, mesh=mesh, in_specs=placed, out_specs=P("gx", "gy", None), check_vma=False
    )
```

```python
import functools

import jax
import jax.numpy as jnp
from jax import lax
from jax.experimental import pallas as pl
from jax.experimental.pallas import tpu as pltpu
from jax.sharding import PartitionSpec as P


CELLS = 8
LANES = 128
ROWS = 4
NEAR = 5
LIMIT = 16 << 20


def call(kernel, out_shape, scratch_shapes=(), far_in=(), far_out=()):
    near = pl.BlockSpec(memory_space=pltpu.VMEM)
    far = pl.BlockSpec(memory_space=pltpu.HBM)

    def run(*operands):
        operands = [
            pltpu.with_memory_space_constraint(x, pltpu.HBM) if k in far_in else x
            for k, x in enumerate(operands)
        ]
        outs = near
        if isinstance(out_shape, list):
            outs = [far if k in far_out else near for k in range(len(out_shape))]
        return pl.pallas_call(
            kernel,
            out_shape=out_shape,
            in_specs=[far if k in far_in else near for k in range(len(operands))],
            out_specs=outs,
            scratch_shapes=list(scratch_shapes),
            compiler_params=pltpu.CompilerParams(vmem_limit_bytes=LIMIT),
        )(*operands)

    return run


def struct(*shape):
    return jax.ShapeDtypeStruct(shape, jnp.float32)


def begin(pairs, sem):
    copies = [pltpu.make_async_copy(*pair, sem.at[k]) for k, pair in enumerate(pairs)]
    for copy in copies:
        copy.start()
    return copies


def copied(values, source_of, width):
    high = values.astype(jnp.bfloat16)
    rest = values - high.astype(jnp.float32)
    middle = rest.astype(jnp.bfloat16)
    low = (rest - middle.astype(jnp.float32)).astype(jnp.bfloat16)
    count = values.shape[1]
    lane = lax.broadcasted_iota(jnp.int32, (3 * count, width), 1)
    row = lax.broadcasted_iota(jnp.int32, (3 * count, width), 0)
    same = (source_of(lane) == lax.rem(row, count)).astype(jnp.bfloat16)
    parts = jnp.concatenate([high, middle, low], axis=1)
    return jnp.dot(parts, same, preferred_element_type=jnp.float32)


def species_scale(diffusivity, width, depth):
    inverse = jnp.broadcast_to(1.0 / diffusivity, (2 * CELLS, width // depth))
    return copied(inverse, lambda lane: lax.div(lane, depth), width)[:CELLS]


def cell_rates(cond, scale, depth):
    width = scale.shape[1]
    inverse = (1.0 / cond).reshape(-1, depth)
    tiles = copied(inverse, lambda lane: lax.rem(lane, depth), width).reshape(CELLS, CELLS, width)
    return [tiles[cell] * scale for cell in range(CELLS)]


def shoot(rates, value, step, order):
    values = [None] * CELLS
    for cell in order:
        values[cell] = value
        step = step + rates[cell] * value
        value = value + step
    return values, value, step


def factors(rates):
    one = jnp.ones_like(rates[0])
    left, out, _ = shoot(rates, one, one, range(CELLS))
    right, _, _ = shoot(rates, one, one, reversed(range(CELLS)))
    inverse = 1.0 / out
    return [value * inverse for value in right], [value * inverse for value in left]


def local_solution(sources, to_first, to_last):
    scale = 1.0 / to_first[CELLS - 1]
    before, after = [None] * CELLS, [None] * CELLS
    running = to_last[0] * sources[0]
    for k in range(CELLS):
        running = running if k == 0 else running + to_last[k] * sources[k]
        before[k] = running
    running = jnp.zeros_like(scale)
    for k in reversed(range(CELLS)):
        after[k] = running
        running = running + to_first[k] * sources[k]
    return [(to_first[k] * before[k] + to_last[k] * after[k]) * scale for k in range(CELLS)]


def total(weights, sources):
    terms = [weight * source for weight, source in zip(weights, sources, strict=True)]
    while len(terms) > 1:
        terms = [a + b for a, b in zip(terms[::2], terms[1::2], strict=True)]
    return terms[0]


def put_rows(send_ref, rows):
    for row, value in enumerate(rows):
        for tile in range(4):
            part = value
            if value.shape[1] > LANES:
                part = value[:, tile * LANES : (tile + 1) * LANES]
            send_ref[pl.ds(tile * ROWS + row, CELLS, stride=4 * ROWS), :] = part


def pack(cond):
    return jnp.concatenate([cond[cell] for cell in range(CELLS)], axis=1)


def get_ends(back_ref):
    return [
        jnp.concatenate(
            [back_ref[pl.ds(tile * 2 + side, CELLS, stride=CELLS), :] for tile in range(4)], axis=1
        )
        for side in range(2)
    ]


def start_kernel(
    depth, cot_from, cond_from, diffusivity_from, send_ref, scale_ref, cot_ref, cond_ref,
    diffusivity_ref, sem,
):
    width = cot_ref.shape[2]
    copies = begin(
        [
            (cond_from, cond_ref),
            (diffusivity_from, diffusivity_ref),
            *((cot_from.at[pl.ds(k, 2)], cot_ref.at[pl.ds(k, 2)]) for k in range(0, CELLS, 2)),
        ],
        sem,
    )
    copies[0].wait()
    copies[1].wait()
    cond = jnp.swapaxes(cond_ref[...], 0, 1)
    scale = species_scale(diffusivity_ref[...], width, depth)
    to_first, to_last = factors(cell_rates(cond, scale, depth))
    packed = pack(cond)
    for tile in range(4):
        scale_ref[pl.ds(tile, 1), :] = scale[0:1, tile * LANES : (tile + 1) * LANES]
    for copy in copies[2:]:
        copy.wait()
    lines = jnp.swapaxes(cot_ref[...], 0, 1)
    sources = [lines[cell] for cell in range(CELLS)]
    put_rows(
        send_ref,
        [total(to_first, sources), total(to_last, sources), packed, jnp.zeros_like(packed)],
    )


def solve_kernel(depth, axis, blocks, tiles, got_ref, scale_ref, out_ref, *scratch):
    value_l, step_l, value_r, step_r, ratio_l, add_l, ratio_r, add_r, sum_l, sum_r = scratch[:10]
    moves, joined = scratch[10:14], scratch[14:]
    pairs = blocks // 2
    even, odd, after = (pl.ds(start, pairs, stride=2) for start in range(3))
    me = lax.axis_index(axis)
    one = jnp.ones((1, LANES), jnp.float32)

    def whole(tile, row):
        return got_ref[pl.ds(tile * ROWS + row, blocks, stride=ROWS * tiles), :]

    for tile in range(tiles):
        scale = scale_ref[pl.ds(lax.rem(me * tiles + tile, 4), 1), :]
        inverse = 1.0 / whole(tile, 2)
        lane = lax.rem(lax.broadcasted_iota(jnp.int32, inverse.shape, 1), depth)
        rates = [
            jnp.take_along_axis(
                inverse, lane + cell * depth, axis=1, mode="promise_in_bounds"
            )
            * scale
            for cell in range(CELLS)
        ]
        ones = jnp.ones_like(inverse)
        flat, _, flat_step = shoot(rates, ones, ones * 0.0, range(CELLS))
        slope, _, slope_step = shoot(rates, ones * 0.0, ones, range(CELLS))
        last = CELLS - 1
        for move, value in zip(moves, (flat_step, slope_step, flat[last], slope[last]), strict=True):
            move[tile] = value
        c0, d0, e0, f0 = (move[tile, even, :] for move in moves)
        c1, d1, e1, f1 = (move[tile, odd, :] for move in moves)
        a0, b0 = c0 + e0, d0 + f0
        joined[0][tile] = c1 * a0 + d1 * c0
        joined[1][tile] = c1 * b0 + d1 * d0
        joined[2][tile] = e1 * a0 + f1 * c0
        joined[3][tile] = e1 * b0 + f1 * d0

    def onward(state, move):
        value, step = state
        c, d, e, f = move
        following = c * value + d * step
        return following + (e * value + f * step), following

    lefts = [(one, one)] * tiles
    rights = [(one, one)] * tiles
    for pair in range(pairs):
        mirror = pairs - 1 - pair
        for tile in range(tiles):
            left, right = lefts[tile], rights[tile]
            value_l[tile, pl.ds(2 * pair, 1), :], step_l[tile, pl.ds(2 * pair, 1), :] = left
            row = pl.ds(2 * mirror + 2, 1)
            value_r[tile, row, :], step_r[tile, row, :] = right
            c, d, e, f = (move[tile, pl.ds(pair, 1), :] for move in joined)
            lefts[tile] = onward(left, (c, d, e, f))
            c, d, e, f = (move[tile, pl.ds(mirror, 1), :] for move in joined)
            rights[tile] = onward(right, (c, e, d, f))
    for tile in range(tiles):
        row = pl.ds(blocks, 1)
        value_l[tile, row, :], step_l[tile, row, :] = lefts[tile]
        row = pl.ds(0, 1)
        value_r[tile, row, :], step_r[tile, row, :] = rights[tile]
        state = value_l[tile, even, :], step_l[tile, even, :]
        state = onward(state, tuple(move[tile, even, :] for move in moves))
        value_l[tile, odd, :], step_l[tile, odd, :] = state
        state = value_r[tile, after, :], step_r[tile, after, :]
        c, d, e, f = (move[tile, odd, :] for move in moves)
        value_r[tile, odd, :], step_r[tile, odd, :] = onward(state, (c, e, d, f))
    for tile in range(tiles):
        near = pl.ds(0, blocks)
        far = pl.ds(1, blocks)
        first, last = whole(tile, 0), whole(tile, 1)
        inverse = 1.0 / value_l[tile, far, :]
        at = value_l[tile, near, :]
        ratio_l[tile] = at * inverse
        add_l[tile] = last + (at - step_l[tile, near, :]) * inverse * first
        inverse = 1.0 / value_r[tile, near, :]
        at = value_r[tile, far, :]
        ratio_r[tile] = at * inverse
        add_r[tile] = first + (at - step_r[tile, far, :]) * inverse * last
        before, behind = ratio_l[tile, odd, :], ratio_r[tile, even, :]
        joined[0][tile] = before * ratio_l[tile, even, :]
        joined[1][tile] = before * add_l[tile, even, :] + add_l[tile, odd, :]
        joined[2][tile] = behind * ratio_r[tile, odd, :]
        joined[3][tile] = behind * add_r[tile, odd, :] + add_r[tile, even, :]
    lefts = [jnp.zeros_like(one)] * tiles
    rights = [jnp.zeros_like(one)] * tiles
    for pair in range(pairs):
        here, there = pl.ds(pair, 1), pl.ds(pairs - 1 - pair, 1)
        for tile in range(tiles):
            sum_l[tile, pl.ds(2 * pair, 1), :] = lefts[tile]
            sum_r[tile, pl.ds(blocks - 2 * pair, 1), :] = rights[tile]
            lefts[tile] = joined[0][tile, here, :] * lefts[tile] + joined[1][tile, here, :]
            rights[tile] = joined[2][tile, there, :] * rights[tile] + joined[3][tile, there, :]
    for tile in range(tiles):
        sum_l[tile, pl.ds(blocks, 1), :] = lefts[tile]
        sum_r[tile, pl.ds(0, 1), :] = rights[tile]
        sum_l[tile, odd, :] = (
            ratio_l[tile, even, :] * sum_l[tile, even, :] + add_l[tile, even, :]
        )
        sum_r[tile, odd, :] = ratio_r[tile, odd, :] * sum_r[tile, after, :] + add_r[tile, odd, :]
    for tile in range(tiles):
        for side in range(2):
            rows = pl.ds(side, blocks)
            gap_l = step_l[tile, rows, :] / value_l[tile, rows, :]
            gap_r = step_r[tile, rows, :] / value_r[tile, rows, :]
            inverse = 1.0 / (gap_l + gap_r * (1.0 - gap_l))
            left, right = sum_l[tile, rows, :], sum_r[tile, rows, :]
            if side == 0:
                ends = (left + (1.0 - gap_l) * right) * inverse
            else:
                ends = (right + (1.0 - gap_r) * left) * inverse
            out_ref[pl.ds(tile * 2 + side, blocks, stride=2 * tiles), :] = ends


def to_species(cells, turn_ref, depth):
    rows = cells.shape[0]
    turn_ref[...] = jnp.concatenate([cells, cells], axis=0).T
    species = cells.shape[1] // depth
    low = lax.broadcasted_iota(jnp.int32, (species, 2 * rows), 1) < rows
    pairs = []
    for pair in range(depth // 2):
        even = turn_ref[pl.ds(2 * pair, species, stride=depth), :]
        odd = turn_ref[pl.ds(2 * pair + 1, species, stride=depth), :]
        pairs.append(jnp.where(low, even, odd))
    return pairs


def from_species(pairs, turn_ref, depth):
    species, columns = pairs[0].shape
    for pair, tile in enumerate(pairs):
        turn_ref[pl.ds(2 * pair, species, stride=depth), :] = tile
        turn_ref[pl.ds(2 * pair + 1, species, stride=depth), :] = pltpu.roll(
            tile, columns // 2, 1
        )
    return turn_ref[...].T[: columns // 2]


def halves(value):
    high = value.astype(jnp.bfloat16)
    return high, (value - high.astype(jnp.float32)).astype(jnp.bfloat16)


def counts(pair_ref, species):
    ids = lax.broadcasted_iota(jnp.int32, (pair_ref.shape[0], species), 1)
    return (pair_ref[:, 0:1] == ids).astype(jnp.float32) + (pair_ref[:, 1:2] == ids).astype(
        jnp.float32
    )


def counts(pair_ref, species):
    ids = lax.broadcasted_iota(jnp.int32, (species, pair_ref.shape[1]), 0)
    return (pair_ref[0:1, :] == ids).astype(jnp.float32) + (pair_ref[1:2, :] == ids).astype(
        jnp.float32
    )


def prepare_kernel(
    depth, cot_from, conc_from, cond_from, diffusivity_from, rate_from, reactants_from,
    products_from, jacobian_to, jacobian_near_ref, local_y_ref, ends_y_ref, ends_x_ref,
    rates_x_ref, packed_x_ref, cot_ref, conc_ref, cond_ref, diffusivity_ref, rate_ref,
    reactants_ref, products_ref, turn_ref, rates_ref, pairs_ref, inverse_ref, jacobian_ref,
    in_sem, sem,
):
    inputs = begin(
        [
            (reactants_from, reactants_ref),
            (products_from, products_ref),
            (rate_from, rate_ref),
            (conc_from, conc_ref),
            (cond_from, cond_ref),
            (diffusivity_from, diffusivity_ref),
            (cot_from, cot_ref),
        ],
        in_sem,
    )
    for copy in inputs:
        copy.wait()
    rows_x, rows_y, width = conc_ref.shape
    species = width // depth
    used = counts(reactants_ref, species)
    net = counts(products_ref, species) - used
    for s in range(species):
        product = (net[s : s + 1, :] * used).astype(jnp.bfloat16)
        rows = pl.ds(s * species, species)
        pairs_ref[rows, : used.shape[1]] = product
        pairs_ref[rows, used.shape[1] :] = product
    twice = jnp.concatenate([used, used], axis=0).T.astype(jnp.bfloat16)
    constant = jnp.broadcast_to(rate_ref[...], (LANES, rate_ref.shape[1])).T
    pairs = to_species(conc_ref[...].reshape(rows_x * rows_y, width), turn_ref, depth)
    for pair, conc in enumerate(pairs):
        columns = pl.ds(pair * conc.shape[1], conc.shape[1])
        inverse_ref[:, columns] = 1.0 / conc
        stacked = jnp.concatenate(halves(jnp.log(conc)), axis=0)
        exponent = jnp.dot(twice, stacked, preferred_element_type=jnp.float32)
        rates_ref[:, columns] = jnp.concatenate(halves(constant * jnp.exp(exponent)), axis=0)
    wide = 2 * LANES
    copies = []
    for chunk in range(rates_ref.shape[1] // wide):
        columns = pl.ds(chunk * wide, wide)
        block = jnp.dot(pairs_ref[...], rates_ref[:, columns], preferred_element_type=jnp.float32)
        for part in range(2):
            tile = 2 * chunk + part - jacobian_ref.shape[0]
            here = pl.ds((2 * chunk + part) * LANES, LANES)
            value = block[:, part * LANES : (part + 1) * LANES].reshape(species, species, LANES)
            value = (value * inverse_ref[:, here][None]).reshape(-1, LANES)
            if tile >= 0:
                jacobian_near_ref[tile] = value
                continue
            tile += jacobian_ref.shape[0]
            jacobian_ref[tile] = value
            copies.append(
                pltpu.make_async_copy(jacobian_ref.at[tile], jacobian_to.at[tile], sem.at[tile])
            )
            copies[-1].start()

    cond = cond_ref[...]
    scale = species_scale(diffusivity_ref[...], width, depth)
    packed_x_ref[...] = pack(cond)
    rates = cell_rates(cond, scale, depth)
    to_first, to_last = factors(rates)
    for k in range(CELLS):
        ends_x_ref[0, k] = to_first[k]
        ends_x_ref[1, k] = to_last[k]
        rates_x_ref[k] = rates[k]
    rates = cell_rates(jnp.swapaxes(cond, 0, 1), scale, depth)
    to_first, to_last = factors(rates)
    lines = jnp.swapaxes(cot_ref[...], 0, 1)
    local = local_solution([lines[k] for k in range(CELLS)], to_first, to_last)
    for k in range(CELLS):
        local_y_ref[k] = local[k] * rates[k]
        ends_y_ref[0, k] = to_first[k] * rates[k]
        ends_y_ref[1, k] = to_last[k] * rates[k]
    for copy in copies:
        copy.wait()


def chemistry(field, columns, jacobian_ref, vector_ref):
    species = field.shape[0]

    def transposed(vector):
        vector_ref[:, columns] = vector
        sums = [None] * 4
        for s in range(species):
            row = jnp.broadcast_to(vector_ref[pl.ds(s, 1), columns], vector.shape)
            term = row * jacobian_ref[pl.ds(s * species, species), :]
            sums[s % 4] = term if sums[s % 4] is None else sums[s % 4] + term
        return (sums[0] + sums[1]) + (sums[2] + sums[3])

    third = field + transposed(field) * (1.0 / 3.0)
    second = field + transposed(third) * 0.5
    return field + transposed(second)


def middle_kernel(
    depth, ends_ref, local_ref, ends_y_ref, jacobian_from, jacobian_near_ref, ends_x_ref,
    packed_x_ref, send_ref, sources_ref, turn_ref, vector_ref, jacobian_ref, sem,
):
    width = local_ref.shape[2]
    far = jacobian_ref.shape[0]
    copies = begin(
        [(jacobian_from.at[tile], jacobian_ref.at[tile]) for tile in range(far)], sem
    )
    left, right = get_ends(ends_ref)
    solved = jnp.stack(
        [
            local_ref[k] + ends_y_ref[0, k] * left + ends_y_ref[1, k] * right
            for k in range(CELLS)
        ],
        axis=0,
    )
    solved = jnp.swapaxes(solved, 0, 1).reshape(CELLS * CELLS, width)
    pairs = to_species(solved, turn_ref, depth)
    done = [None] * len(pairs)
    for pair in [*range(far, len(pairs)), *range(far)]:
        field = pairs[pair]
        columns = pl.ds(pair * field.shape[1], field.shape[1])
        if pair < far:
            copies[pair].wait()
            jacobian = jacobian_ref.at[pair]
        else:
            jacobian = jacobian_near_ref.at[pair - far]
        done[pair] = chemistry(field, columns, jacobian, vector_ref)
    changed = from_species(done, turn_ref, depth).reshape(CELLS, CELLS, width)
    sources_ref[...] = changed
    sources = [changed[k] for k in range(CELLS)]
    packed = packed_x_ref[...]
    put_rows(
        send_ref,
        [
            total([ends_x_ref[0, k] for k in range(CELLS)], sources),
            total([ends_x_ref[1, k] for k in range(CELLS)], sources),
            packed,
            jnp.zeros_like(packed),
        ],
    )


def finish_kernel(ends_ref, sources_ref, ends_x_ref, rates_ref, out_to, out_ref, sem):
    to_first = [ends_x_ref[0, k] for k in range(CELLS)]
    to_last = [ends_x_ref[1, k] for k in range(CELLS)]
    local = local_solution([sources_ref[k] for k in range(CELLS)], to_first, to_last)
    left, right = get_ends(ends_ref)
    copies = []
    for k in range(CELLS):
        out_ref[k] = (local[k] + to_first[k] * left + to_last[k] * right) * rates_ref[k]
        if k % 2:
            pair = pl.ds(k - 1, 2)
            copies.append(pltpu.make_async_copy(out_ref.at[pair], out_to.at[pair], sem.at[k // 2]))
            copies[-1].start()
    for copy in copies:
        copy.wait()


def exchange(rows, axis):
    members = lax.axis_size(axis)
    blocks = rows.reshape(members, rows.shape[0] // members, LANES)
    return lax.all_to_all(blocks, axis, 0, 0, tiled=True).reshape(rows.shape)


def solve_lines(send, scale, axis, depth, beside=None):
    blocks = lax.axis_size(axis)
    got = exchange(send, axis)
    if beside is not None:
        got, beside = lax.optimization_barrier((got, beside))
    tiles = send.shape[0] // (blocks * ROWS)
    states = pltpu.VMEM((tiles, blocks + CELLS, LANES), jnp.float32)
    terms = pltpu.VMEM((tiles, blocks, LANES), jnp.float32)
    joins = pltpu.VMEM((tiles, blocks // 2, LANES), jnp.float32)
    ends = call(
        functools.partial(solve_kernel, depth, axis, blocks, tiles),
        struct(2 * blocks * tiles, LANES),
        [states] * 4 + [terms] * 4 + [states] * 2 + [terms] * 4 + [joins] * 4,
    )(got, scale)
    return exchange(ends, axis), beside


def on_device(
    cotangent, concentration, conductance, diffusivity, rate_constant, reactants, products
):
    rows_x, rows_y, width = cotangent.shape
    depth = conductance.shape[2]
    species = diffusivity.shape[0]
    reactions = rate_constant.shape[0]
    columns = rows_x * rows_y * depth
    diffusivity = diffusivity[None, :]
    turn = pltpu.VMEM((width, 2 * rows_x * rows_y), jnp.float32)
    block = struct(CELLS, CELLS, width)
    send = struct(CELLS * (width // LANES) * ROWS, LANES)

    send_y, scale = call(
        functools.partial(start_kernel, depth),
        [send, struct(CELLS, LANES)],
        [
            pltpu.VMEM(cotangent.shape, jnp.float32),
            pltpu.VMEM(conductance.shape, jnp.float32),
            pltpu.VMEM(diffusivity.shape, jnp.float32),
            pltpu.SemaphoreType.DMA((6,)),
        ],
        far_in=(0, 1, 2),
    )(cotangent, conductance, diffusivity)
    count = columns // LANES
    tile = (species * species, LANES)
    jacobian, jacobian_near, local_y, ends_y, ends_x, rates_x, packed_x = call(
        functools.partial(prepare_kernel, depth),
        [
            pltpu.HBM((count - NEAR, *tile), jnp.float32),
            struct(NEAR, *tile),
            block,
            struct(2, CELLS, CELLS, width),
            struct(2, CELLS, CELLS, width),
            block,
            struct(CELLS, LANES),
        ],
        [
            pltpu.VMEM(cotangent.shape, jnp.float32),
            pltpu.VMEM(concentration.shape, jnp.float32),
            pltpu.VMEM(conductance.shape, jnp.float32),
            pltpu.VMEM(diffusivity.shape, jnp.float32),
            pltpu.VMEM((1, reactions), jnp.float32),
            pltpu.VMEM((2, reactions), jnp.int32),
            pltpu.VMEM((2, reactions), jnp.int32),
            turn,
            pltpu.VMEM((2 * reactions, columns), jnp.bfloat16),
            pltpu.VMEM((species * species, 2 * reactions), jnp.bfloat16),
            pltpu.VMEM((species, columns), jnp.float32),
            pltpu.VMEM((count - NEAR, *tile), jnp.float32),
            pltpu.SemaphoreType.DMA((7,)),
            pltpu.SemaphoreType.DMA((count - NEAR,)),
        ],
        far_in=tuple(range(7)),
        far_out=(0,),
    )(
        cotangent,
        concentration,
        conductance,
        diffusivity,
        rate_constant[None, :],
        reactants.T,
        products.T,
    )
    got_y, packed_x = solve_lines(send_y, scale, "gy", depth, packed_x)
    send_x, sources = call(
        functools.partial(middle_kernel, depth),
        [send, block],
        [
            turn,
            pltpu.VMEM((species, columns), jnp.float32),
            pltpu.VMEM((count - NEAR, *tile), jnp.float32),
            pltpu.SemaphoreType.DMA((count - NEAR,)),
        ],
        far_in=(3,),
    )(got_y, local_y, ends_y, jacobian, jacobian_near, ends_x, packed_x)
    got_x, _ = solve_lines(send_x, scale, "gx", depth)
    return call(
        finish_kernel,
        [block],
        [pltpu.VMEM(block.shape, jnp.float32), pltpu.SemaphoreType.DMA((CELLS // 2,))],
        far_out=(0,),
    )(got_x, sources, ends_x, rates_x)[0]


def solution(mesh):
    placed = (P("gx", "gy", None), P("gx", "gy", None), P("gx", "gy", None), P(), P(), P(), P())
    return jax.shard_map(
        on_device, mesh=mesh, in_specs=placed, out_specs=P("gx", "gy", None), check_vma=False
    )
```

```python
import functools

import jax
import jax.numpy as jnp
from jax import lax
from jax.experimental import pallas as pl
from jax.experimental.pallas import tpu as pltpu
from jax.sharding import PartitionSpec as P


CELLS = 8
LANES = 128
ROWS = 4
NEAR = 5
LIMIT = 16 << 20


def call(kernel, out_shape, scratch_shapes=(), far_in=(), far_out=()):
    near = pl.BlockSpec(memory_space=pltpu.VMEM)
    far = pl.BlockSpec(memory_space=pltpu.HBM)

    def run(*operands):
        operands = [
            pltpu.with_memory_space_constraint(x, pltpu.HBM) if k in far_in else x
            for k, x in enumerate(operands)
        ]
        outs = near
        if isinstance(out_shape, list):
            outs = [far if k in far_out else near for k in range(len(out_shape))]
        return pl.pallas_call(
            kernel,
            out_shape=out_shape,
            in_specs=[far if k in far_in else near for k in range(len(operands))],
            out_specs=outs,
            scratch_shapes=list(scratch_shapes),
            compiler_params=pltpu.CompilerParams(vmem_limit_bytes=LIMIT),
        )(*operands)

    return run


def struct(*shape):
    return jax.ShapeDtypeStruct(shape, jnp.float32)


def begin(pairs, sem):
    copies = [pltpu.make_async_copy(*pair, sem.at[k]) for k, pair in enumerate(pairs)]
    for copy in copies:
        copy.start()
    return copies


def copied(values, source_of, width):
    high = values.astype(jnp.bfloat16)
    rest = values - high.astype(jnp.float32)
    middle = rest.astype(jnp.bfloat16)
    low = (rest - middle.astype(jnp.float32)).astype(jnp.bfloat16)
    count = values.shape[1]
    lane = lax.broadcasted_iota(jnp.int32, (3 * count, width), 1)
    row = lax.broadcasted_iota(jnp.int32, (3 * count, width), 0)
    same = (source_of(lane) == lax.rem(row, count)).astype(jnp.bfloat16)
    parts = jnp.concatenate([high, middle, low], axis=1)
    return jnp.dot(parts, same, preferred_element_type=jnp.float32)


def species_scale(diffusivity, width, depth):
    inverse = jnp.broadcast_to(1.0 / diffusivity, (2 * CELLS, width // depth))
    return copied(inverse, lambda lane: lax.div(lane, depth), width)[:CELLS]


def cell_rates(cond, scale, depth):
    width = scale.shape[1]
    inverse = (1.0 / cond).reshape(-1, depth)
    tiles = copied(inverse, lambda lane: lax.rem(lane, depth), width).reshape(CELLS, CELLS, width)
    return [tiles[cell] * scale for cell in range(CELLS)]


def shoot(rates, value, step, order):
    values = [None] * CELLS
    for cell in order:
        values[cell] = value
        step = step + rates[cell] * value
        value = value + step
    return values, value, step


def factors(rates):
    one = jnp.ones_like(rates[0])
    left, out, _ = shoot(rates, one, one, range(CELLS))
    right, _, _ = shoot(rates, one, one, reversed(range(CELLS)))
    inverse = 1.0 / out
    return [value * inverse for value in right], [value * inverse for value in left]


def local_solution(sources, to_first, to_last):
    scale = 1.0 / to_first[CELLS - 1]
    before, after = [None] * CELLS, [None] * CELLS
    running = to_last[0] * sources[0]
    for k in range(CELLS):
        running = running if k == 0 else running + to_last[k] * sources[k]
        before[k] = running
    running = jnp.zeros_like(scale)
    for k in reversed(range(CELLS)):
        after[k] = running
        running = running + to_first[k] * sources[k]
    return [(to_first[k] * before[k] + to_last[k] * after[k]) * scale for k in range(CELLS)]


def total(weights, sources):
    terms = [weight * source for weight, source in zip(weights, sources, strict=True)]
    while len(terms) > 1:
        terms = [a + b for a, b in zip(terms[::2], terms[1::2], strict=True)]
    return terms[0]


def put_rows(send_ref, rows):
    for row, value in enumerate(rows):
        for tile in range(4):
            part = value
            if value.shape[1] > LANES:
                part = value[:, tile * LANES : (tile + 1) * LANES]
            send_ref[pl.ds(tile * ROWS + row, CELLS, stride=4 * ROWS), :] = part


def pack(cond):
    return jnp.concatenate([cond[cell] for cell in range(CELLS)], axis=1)


def get_ends(back_ref):
    return [
        jnp.concatenate(
            [back_ref[pl.ds(tile * 2 + side, CELLS, stride=CELLS), :] for tile in range(4)], axis=1
        )
        for side in range(2)
    ]


def start_kernel(
    depth, cot_from, cond_from, diffusivity_from, send_ref, scale_ref, cot_ref, cond_ref,
    diffusivity_ref, sem,
):
    width = cot_ref.shape[2]
    copies = begin(
        [
            (cond_from, cond_ref),
            (diffusivity_from, diffusivity_ref),
            (cot_from, cot_ref),
        ],
        sem,
    )
    copies[0].wait()
    copies[1].wait()
    cond = jnp.swapaxes(cond_ref[...], 0, 1)
    scale = species_scale(diffusivity_ref[...], width, depth)
    to_first, to_last = factors(cell_rates(cond, scale, depth))
    packed = pack(cond)
    for tile in range(4):
        scale_ref[pl.ds(tile, 1), :] = scale[0:1, tile * LANES : (tile + 1) * LANES]
    for copy in copies[2:]:
        copy.wait()
    lines = jnp.swapaxes(cot_ref[...], 0, 1)
    sources = [lines[cell] for cell in range(CELLS)]
    put_rows(
        send_ref,
        [total(to_first, sources), total(to_last, sources), packed, jnp.zeros_like(packed)],
    )


def solve_kernel(depth, axis, blocks, tiles, got_ref, scale_ref, out_ref, *scratch):
    value_l, step_l, value_r, step_r, ratio_l, add_l, ratio_r, add_r, sum_l, sum_r = scratch[:10]
    moves, joined = scratch[10:14], scratch[14:]
    pairs = blocks // 2
    even, odd, after = (pl.ds(start, pairs, stride=2) for start in range(3))
    me = lax.axis_index(axis)
    one = jnp.ones((1, LANES), jnp.float32)

    def whole(tile, row):
        return got_ref[pl.ds(tile * ROWS + row, blocks, stride=ROWS * tiles), :]

    for tile in range(tiles):
        scale = scale_ref[pl.ds(lax.rem(me * tiles + tile, 4), 1), :]
        inverse = 1.0 / whole(tile, 2)
        lane = lax.rem(lax.broadcasted_iota(jnp.int32, inverse.shape, 1), depth)
        rates = [
            jnp.take_along_axis(
                inverse, lane + cell * depth, axis=1, mode="promise_in_bounds"
            )
            * scale
            for cell in range(CELLS)
        ]
        ones = jnp.ones_like(inverse)
        flat, _, flat_step = shoot(rates, ones, ones * 0.0, range(CELLS))
        slope, _, slope_step = shoot(rates, ones * 0.0, ones, range(CELLS))
        last = CELLS - 1
        for move, value in zip(moves, (flat_step, slope_step, flat[last], slope[last]), strict=True):
            move[tile] = value
        c0, d0, e0, f0 = (move[tile, even, :] for move in moves)
        c1, d1, e1, f1 = (move[tile, odd, :] for move in moves)
        a0, b0 = c0 + e0, d0 + f0
        joined[0][tile] = c1 * a0 + d1 * c0
        joined[1][tile] = c1 * b0 + d1 * d0
        joined[2][tile] = e1 * a0 + f1 * c0
        joined[3][tile] = e1 * b0 + f1 * d0

    def onward(state, move):
        value, step = state
        c, d, e, f = move
        following = c * value + d * step
        return following + (e * value + f * step), following

    lefts = [(one, one)] * tiles
    rights = [(one, one)] * tiles
    for pair in range(pairs):
        mirror = pairs - 1 - pair
        for tile in range(tiles):
            left, right = lefts[tile], rights[tile]
            value_l[tile, pl.ds(2 * pair, 1), :], step_l[tile, pl.ds(2 * pair, 1), :] = left
            row = pl.ds(2 * mirror + 2, 1)
            value_r[tile, row, :], step_r[tile, row, :] = right
            c, d, e, f = (move[tile, pl.ds(pair, 1), :] for move in joined)
            lefts[tile] = onward(left, (c, d, e, f))
            c, d, e, f = (move[tile, pl.ds(mirror, 1), :] for move in joined)
            rights[tile] = onward(right, (c, e, d, f))
    for tile in range(tiles):
        row = pl.ds(blocks, 1)
        value_l[tile, row, :], step_l[tile, row, :] = lefts[tile]
        row = pl.ds(0, 1)
        value_r[tile, row, :], step_r[tile, row, :] = rights[tile]
        state = value_l[tile, even, :], step_l[tile, even, :]
        state = onward(state, tuple(move[tile, even, :] for move in moves))
        value_l[tile, odd, :], step_l[tile, odd, :] = state
        state = value_r[tile, after, :], step_r[tile, after, :]
        c, d, e, f = (move[tile, odd, :] for move in moves)
        value_r[tile, odd, :], step_r[tile, odd, :] = onward(state, (c, e, d, f))
    for tile in range(tiles):
        near = pl.ds(0, blocks)
        far = pl.ds(1, blocks)
        first, last = whole(tile, 0), whole(tile, 1)
        inverse = 1.0 / value_l[tile, far, :]
        at = value_l[tile, near, :]
        ratio_l[tile] = at * inverse
        add_l[tile] = last + (at - step_l[tile, near, :]) * inverse * first
        inverse = 1.0 / value_r[tile, near, :]
        at = value_r[tile, far, :]
        ratio_r[tile] = at * inverse
        add_r[tile] = first + (at - step_r[tile, far, :]) * inverse * last
        before, behind = ratio_l[tile, odd, :], ratio_r[tile, even, :]
        joined[0][tile] = before * ratio_l[tile, even, :]
        joined[1][tile] = before * add_l[tile, even, :] + add_l[tile, odd, :]
        joined[2][tile] = behind * ratio_r[tile, odd, :]
        joined[3][tile] = behind * add_r[tile, odd, :] + add_r[tile, even, :]
    lefts = [jnp.zeros_like(one)] * tiles
    rights = [jnp.zeros_like(one)] * tiles
    for pair in range(pairs):
        here, there = pl.ds(pair, 1), pl.ds(pairs - 1 - pair, 1)
        for tile in range(tiles):
            sum_l[tile, pl.ds(2 * pair, 1), :] = lefts[tile]
            sum_r[tile, pl.ds(blocks - 2 * pair, 1), :] = rights[tile]
            lefts[tile] = joined[0][tile, here, :] * lefts[tile] + joined[1][tile, here, :]
            rights[tile] = joined[2][tile, there, :] * rights[tile] + joined[3][tile, there, :]
    for tile in range(tiles):
        sum_l[tile, pl.ds(blocks, 1), :] = lefts[tile]
        sum_r[tile, pl.ds(0, 1), :] = rights[tile]
        sum_l[tile, odd, :] = (
            ratio_l[tile, even, :] * sum_l[tile, even, :] + add_l[tile, even, :]
        )
        sum_r[tile, odd, :] = ratio_r[tile, odd, :] * sum_r[tile, after, :] + add_r[tile, odd, :]
    for tile in range(tiles):
        for side in range(2):
            rows = pl.ds(side, blocks)
            gap_l = step_l[tile, rows, :] / value_l[tile, rows, :]
            gap_r = step_r[tile, rows, :] / value_r[tile, rows, :]
            inverse = 1.0 / (gap_l + gap_r * (1.0 - gap_l))
            left, right = sum_l[tile, rows, :], sum_r[tile, rows, :]
            if side == 0:
                ends = (left + (1.0 - gap_l) * right) * inverse
            else:
                ends = (right + (1.0 - gap_r) * left) * inverse
            out_ref[pl.ds(tile * 2 + side, blocks, stride=2 * tiles), :] = ends


def to_species(cells, turn_ref, depth):
    rows = cells.shape[0]
    turn_ref[...] = jnp.concatenate([cells, cells], axis=0).T
    species = cells.shape[1] // depth
    low = lax.broadcasted_iota(jnp.int32, (species, 2 * rows), 1) < rows
    pairs = []
    for pair in range(depth // 2):
        even = turn_ref[pl.ds(2 * pair, species, stride=depth), :]
        odd = turn_ref[pl.ds(2 * pair + 1, species, stride=depth), :]
        pairs.append(jnp.where(low, even, odd))
    return pairs


def from_species(pairs, turn_ref, depth):
    species, columns = pairs[0].shape
    for pair, tile in enumerate(pairs):
        turn_ref[pl.ds(2 * pair, species, stride=depth), :] = tile
        turn_ref[pl.ds(2 * pair + 1, species, stride=depth), :] = pltpu.roll(
            tile, columns // 2, 1
        )
    return turn_ref[...].T[: columns // 2]


def halves(value):
    high = value.astype(jnp.bfloat16)
    return high, (value - high.astype(jnp.float32)).astype(jnp.bfloat16)


def counts(pair_ref, species):
    ids = lax.broadcasted_iota(jnp.int32, (pair_ref.shape[0], species), 1)
    return (pair_ref[:, 0:1] == ids).astype(jnp.float32) + (pair_ref[:, 1:2] == ids).astype(
        jnp.float32
    )


def counts(pair_ref, species):
    ids = lax.broadcasted_iota(jnp.int32, (species, pair_ref.shape[1]), 0)
    return (pair_ref[0:1, :] == ids).astype(jnp.float32) + (pair_ref[1:2, :] == ids).astype(
        jnp.float32
    )


def prepare_kernel(
    depth, cot_from, conc_from, cond_from, diffusivity_from, rate_from, reactants_from,
    products_from, jacobian_to, jacobian_near_ref, local_y_ref, ends_y_ref, ends_x_ref,
    rates_x_ref, packed_x_ref, cot_ref, conc_ref, cond_ref, diffusivity_ref, rate_ref,
    reactants_ref, products_ref, turn_ref, rates_ref, pairs_ref, inverse_ref, jacobian_ref,
    in_sem, sem,
):
    inputs = begin(
        [
            (reactants_from, reactants_ref),
            (products_from, products_ref),
            (rate_from, rate_ref),
            (conc_from, conc_ref),
            (cond_from, cond_ref),
            (diffusivity_from, diffusivity_ref),
            (cot_from, cot_ref),
        ],
        in_sem,
    )
    for copy in inputs:
        copy.wait()
    rows_x, rows_y, width = conc_ref.shape
    species = width // depth
    used = counts(reactants_ref, species)
    net = counts(products_ref, species) - used
    for s in range(species):
        product = (net[s : s + 1, :] * used).astype(jnp.bfloat16)
        rows = pl.ds(s * species, species)
        pairs_ref[rows, : used.shape[1]] = product
        pairs_ref[rows, used.shape[1] :] = product
    twice = jnp.concatenate([used, used], axis=0).T.astype(jnp.bfloat16)
    constant = jnp.broadcast_to(rate_ref[...], (LANES, rate_ref.shape[1])).T
    pairs = to_species(conc_ref[...].reshape(rows_x * rows_y, width), turn_ref, depth)
    for pair, conc in enumerate(pairs):
        columns = pl.ds(pair * conc.shape[1], conc.shape[1])
        inverse_ref[:, columns] = 1.0 / conc
        stacked = jnp.concatenate(halves(jnp.log(conc)), axis=0)
        exponent = jnp.dot(twice, stacked, preferred_element_type=jnp.float32)
        rates_ref[:, columns] = jnp.concatenate(halves(constant * jnp.exp(exponent)), axis=0)
    wide = 2 * LANES
    copies = []
    for chunk in range(rates_ref.shape[1] // wide):
        columns = pl.ds(chunk * wide, wide)
        block = jnp.dot(pairs_ref[...], rates_ref[:, columns], preferred_element_type=jnp.float32)
        for part in range(2):
            tile = 2 * chunk + part - jacobian_ref.shape[0]
            here = pl.ds((2 * chunk + part) * LANES, LANES)
            value = block[:, part * LANES : (part + 1) * LANES].reshape(species, species, LANES)
            value = (value * inverse_ref[:, here][None]).reshape(-1, LANES)
            if tile >= 0:
                jacobian_near_ref[tile] = value
                continue
            tile += jacobian_ref.shape[0]
            jacobian_ref[tile] = value
            copies.append(
                pltpu.make_async_copy(jacobian_ref.at[tile], jacobian_to.at[tile], sem.at[tile])
            )
            copies[-1].start()

    cond = cond_ref[...]
    scale = species_scale(diffusivity_ref[...], width, depth)
    packed_x_ref[...] = pack(cond)
    rates = cell_rates(cond, scale, depth)
    to_first, to_last = factors(rates)
    for k in range(CELLS):
        ends_x_ref[0, k] = to_first[k]
        ends_x_ref[1, k] = to_last[k]
        rates_x_ref[k] = rates[k]
    rates = cell_rates(jnp.swapaxes(cond, 0, 1), scale, depth)
    to_first, to_last = factors(rates)
    lines = jnp.swapaxes(cot_ref[...], 0, 1)
    local = local_solution([lines[k] for k in range(CELLS)], to_first, to_last)
    for k in range(CELLS):
        local_y_ref[k] = local[k] * rates[k]
        ends_y_ref[0, k] = to_first[k] * rates[k]
        ends_y_ref[1, k] = to_last[k] * rates[k]
    for copy in copies:
        copy.wait()


def chemistry(field, columns, jacobian_ref, vector_ref):
    species = field.shape[0]

    def transposed(vector):
        vector_ref[:, columns] = vector
        sums = [None] * 4
        for s in range(species):
            row = jnp.broadcast_to(vector_ref[pl.ds(s, 1), columns], vector.shape)
            term = row * jacobian_ref[pl.ds(s * species, species), :]
            sums[s % 4] = term if sums[s % 4] is None else sums[s % 4] + term
        return (sums[0] + sums[1]) + (sums[2] + sums[3])

    third = field + transposed(field) * (1.0 / 3.0)
    second = field + transposed(third) * 0.5
    return field + transposed(second)


def middle_kernel(
    depth, ends_ref, local_ref, ends_y_ref, jacobian_from, jacobian_near_ref, ends_x_ref,
    packed_x_ref, send_ref, sources_ref, turn_ref, vector_ref, jacobian_ref, sem,
):
    width = local_ref.shape[2]
    far = jacobian_ref.shape[0]
    copies = begin(
        [(jacobian_from.at[tile], jacobian_ref.at[tile]) for tile in range(far)], sem
    )
    left, right = get_ends(ends_ref)
    solved = jnp.stack(
        [
            local_ref[k] + ends_y_ref[0, k] * left + ends_y_ref[1, k] * right
            for k in range(CELLS)
        ],
        axis=0,
    )
    solved = jnp.swapaxes(solved, 0, 1).reshape(CELLS * CELLS, width)
    pairs = to_species(solved, turn_ref, depth)
    done = [None] * len(pairs)
    for pair in [*range(far, len(pairs)), *range(far)]:
        field = pairs[pair]
        columns = pl.ds(pair * field.shape[1], field.shape[1])
        if pair < far:
            copies[pair].wait()
            jacobian = jacobian_ref.at[pair]
        else:
            jacobian = jacobian_near_ref.at[pair - far]
        done[pair] = chemistry(field, columns, jacobian, vector_ref)
    changed = from_species(done, turn_ref, depth).reshape(CELLS, CELLS, width)
    sources_ref[...] = changed
    sources = [changed[k] for k in range(CELLS)]
    packed = packed_x_ref[...]
    put_rows(
        send_ref,
        [
            total([ends_x_ref[0, k] for k in range(CELLS)], sources),
            total([ends_x_ref[1, k] for k in range(CELLS)], sources),
            packed,
            jnp.zeros_like(packed),
        ],
    )


def finish_kernel(ends_ref, sources_ref, ends_x_ref, rates_ref, out_ref):
    to_first = [ends_x_ref[0, k] for k in range(CELLS)]
    to_last = [ends_x_ref[1, k] for k in range(CELLS)]
    local = local_solution([sources_ref[k] for k in range(CELLS)], to_first, to_last)
    left, right = get_ends(ends_ref)
    for k in range(CELLS):
        out_ref[k] = (local[k] + to_first[k] * left + to_last[k] * right) * rates_ref[k]


def exchange(rows, axis):
    members = lax.axis_size(axis)
    blocks = rows.reshape(members, rows.shape[0] // members, LANES)
    return lax.all_to_all(blocks, axis, 0, 0, tiled=True).reshape(rows.shape)


def solve_lines(send, scale, axis, depth, beside=None):
    blocks = lax.axis_size(axis)
    got = exchange(send, axis)
    if beside is not None:
        got, beside = lax.optimization_barrier((got, beside))
    tiles = send.shape[0] // (blocks * ROWS)
    states = pltpu.VMEM((tiles, blocks + CELLS, LANES), jnp.float32)
    terms = pltpu.VMEM((tiles, blocks, LANES), jnp.float32)
    joins = pltpu.VMEM((tiles, blocks // 2, LANES), jnp.float32)
    ends = call(
        functools.partial(solve_kernel, depth, axis, blocks, tiles),
        struct(2 * blocks * tiles, LANES),
        [states] * 4 + [terms] * 4 + [states] * 2 + [terms] * 4 + [joins] * 4,
    )(got, scale)
    return exchange(ends, axis), beside


def on_device(
    cotangent, concentration, conductance, diffusivity, rate_constant, reactants, products
):
    rows_x, rows_y, width = cotangent.shape
    depth = conductance.shape[2]
    species = diffusivity.shape[0]
    reactions = rate_constant.shape[0]
    columns = rows_x * rows_y * depth
    diffusivity = diffusivity[None, :]
    turn = pltpu.VMEM((width, 2 * rows_x * rows_y), jnp.float32)
    block = struct(CELLS, CELLS, width)
    send = struct(CELLS * (width // LANES) * ROWS, LANES)

    send_y, scale = call(
        functools.partial(start_kernel, depth),
        [send, struct(CELLS, LANES)],
        [
            pltpu.VMEM(cotangent.shape, jnp.float32),
            pltpu.VMEM(conductance.shape, jnp.float32),
            pltpu.VMEM(diffusivity.shape, jnp.float32),
            pltpu.SemaphoreType.DMA((3,)),
        ],
        far_in=(0, 1, 2),
    )(cotangent, conductance, diffusivity)
    count = columns // LANES
    tile = (species * species, LANES)
    jacobian, jacobian_near, local_y, ends_y, ends_x, rates_x, packed_x = call(
        functools.partial(prepare_kernel, depth),
        [
            pltpu.HBM((count - NEAR, *tile), jnp.float32),
            struct(NEAR, *tile),
            block,
            struct(2, CELLS, CELLS, width),
            struct(2, CELLS, CELLS, width),
            block,
            struct(CELLS, LANES),
        ],
        [
            pltpu.VMEM(cotangent.shape, jnp.float32),
            pltpu.VMEM(concentration.shape, jnp.float32),
            pltpu.VMEM(conductance.shape, jnp.float32),
            pltpu.VMEM(diffusivity.shape, jnp.float32),
            pltpu.VMEM((1, reactions), jnp.float32),
            pltpu.VMEM((2, reactions), jnp.int32),
            pltpu.VMEM((2, reactions), jnp.int32),
            turn,
            pltpu.VMEM((2 * reactions, columns), jnp.bfloat16),
            pltpu.VMEM((species * species, 2 * reactions), jnp.bfloat16),
            pltpu.VMEM((species, columns), jnp.float32),
            pltpu.VMEM((count - NEAR, *tile), jnp.float32),
            pltpu.SemaphoreType.DMA((7,)),
            pltpu.SemaphoreType.DMA((count - NEAR,)),
        ],
        far_in=tuple(range(7)),
        far_out=(0,),
    )(
        cotangent,
        concentration,
        conductance,
        diffusivity,
        rate_constant[None, :],
        reactants.T,
        products.T,
    )
    got_y, packed_x = solve_lines(send_y, scale, "gy", depth, packed_x)
    send_x, sources = call(
        functools.partial(middle_kernel, depth),
        [send, block],
        [
            turn,
            pltpu.VMEM((species, columns), jnp.float32),
            pltpu.VMEM((count - NEAR, *tile), jnp.float32),
            pltpu.SemaphoreType.DMA((count - NEAR,)),
        ],
        far_in=(3,),
    )(got_y, local_y, ends_y, jacobian, jacobian_near, ends_x, packed_x)
    got_x, _ = solve_lines(send_x, scale, "gx", depth)
    return call(finish_kernel, block)(got_x, sources, ends_x, rates_x)


def solution(mesh):
    placed = (P("gx", "gy", None), P("gx", "gy", None), P("gx", "gy", None), P(), P(), P(), P())
    return jax.shard_map(
        on_device, mesh=mesh, in_specs=placed, out_specs=P("gx", "gy", None), check_vma=False
    )
```
